32 devices in a mesh: dp: 4 (over y, x), seq: 4 (over z), tensor: 2 (over core).
Axes of the slice: x: 2, y: 2, z: 4, core: 2. Of those that a mesh axis runs over, the one named last changes fastest.
Arguments:
- inputs: bfloat16 [2, 4, 2048, 2048], P(None, 'dp', ('seq', 'tensor')), may hold values from -6 to 6
- lengths: int32 [2, 4, 3], P(None, 'dp'), may hold values from 1 to 1536, 2048 in all within a row
- first_gain: bfloat16 [2048], P(('dp', 'seq')), may hold values from 0.5 to 1.5
- second_gain: bfloat16 [2048], P(('dp', 'seq')), may hold values from 0.5 to 1.5
- query_weight: bfloat16 [2048, 2048], P(('dp', 'seq'), 'tensor'), may hold values from -0.125 to 0.125
- key_weight: bfloat16 [2048, 2048], P(('dp', 'seq'), 'tensor'), may hold values from -0.125 to 0.125
- value_weight: bfloat16 [2048, 4096], P(('dp', 'seq'), 'tensor'), may hold values from -0.125 to 0.125
- gate_weight: bfloat16 [2048, 4096], P(('dp', 'seq'), 'tensor'), may hold values from -0.125 to 0.125
- out_weight: bfloat16 [2048, 4096], P(('dp', 'seq'), 'tensor'), may hold values from -0.1875 to 0.1875
- up_weight: bfloat16 [2048, 4096], P(('dp', 'seq'), 'tensor'), may hold values from -0.125 to 0.125
- down_weight: bfloat16 [2048, 4096], P(('dp', 'seq'), 'tensor'), may hold values from -0.125 to 0.125
- out_cotangent: bfloat16 [2, 4, 2048, 2048], P(None, 'dp', ('seq', 'tensor')), may hold values from -6 to 6
Outputs:
- output: bfloat16 [2, 4, 2048, 2048], P(None, 'dp', ('seq', 'tensor'))
- grad_inputs: bfloat16 [2, 4, 2048, 2048], P(None, 'dp', ('seq', 'tensor'))
- grad_first_gain: float32 [2048], P(('dp', 'seq'))
- grad_second_gain: float32 [2048], P(('dp', 'seq'))
- grad_query: float32 [2048, 2048], P(('dp', 'seq'), 'tensor')
- grad_key: float32 [2048, 2048], P(('dp', 'seq'), 'tensor')
- grad_value: float32 [2048, 4096], P(('dp', 'seq'), 'tensor')
- grad_gate: float32 [2048, 4096], P(('dp', 'seq'), 'tensor')
- grad_out: float32 [2048, 4096], P(('dp', 'seq'), 'tensor')
- grad_up: float32 [2048, 4096], P(('dp', 'seq'), 'tensor')
- grad_down: float32 [2048, 4096], P(('dp', 'seq'), 'tensor')
The draws below stay inside these ranges and needn't reach their ends.
Inputs may be any that keep to these rules, and one draw needn't show every extreme that they name: The 3 lengths of a row sum to 2048.
All inputs are finite; a program needn't handle non-finite values.
Results may differ from the reference program's by a relative error of at most 0.024.
Values may be sent and summed in bfloat16 or wider, within the bound.
No kernel may reach another device: no remote copies, remote signals or barrier semaphores. Data moves between devices by JAX's collectives and lax.ppermute only.
A program may use at most 448 MiB of HBM per device.

```python
import math
import jax
import jax.numpy as jnp
import numpy as np
from jax import lax

D = 2048
HEADS = 8
QK = 256
HV = 512
FF = 4096
HQ = 2048
VW = 4096
ROW_LEN = 2048
SEQS = 3
MICRO = 2
ROWS = 4
BLOCK = 512


def with_spikes(drawn, rng, source, target, parts, factor):
    owner, partner = [(jnp.arange(drawn.shape[dim]) // (drawn.shape[dim] // parts)).reshape([-1 if axis == dim else 1 for axis in range(drawn.ndim)]) for dim in (source, target)]
    chosen = jax.random.permutation(rng, parts)[partner]
    strong = (owner == chosen) | (owner == (partner + parts // 2) % parts)
    return jnp.where(strong, factor * drawn, drawn)


def level_of(rng, dims, shards, smallest, largest):
    def one(dim, shards_of):
        draws = jax.random.uniform(jax.random.fold_in(jax.random.fold_in(rng, 6), dim), (shards_of,), jnp.float32, smallest / len(shards), largest / len(shards))
        return jnp.repeat(jnp.exp(draws), dims[dim] // shards_of).reshape((-1,) + (1,) * (len(dims) - dim - 1))

    level = one(*shards[0])
    for cut in shards[1:]:
        level = level * one(*cut)
    return level


def split_up(number_of, total, reach, slope):
    weights = [(1 << 20) // math.isqrt(rank ** slope) + 1 for rank in range(2, number_of + 1)]
    rest, given = total - reach - (number_of - 1), [1] * (number_of - 1)
    while rest > 0:
        candidates = [i for i in range(number_of - 1) if given[i] < reach]
        pool, budget = sum([weights[i] for i in candidates]), rest
        for i in candidates:
            extra = min(reach - given[i], max(1, budget * weights[i] // pool), rest)
            given[i] = given[i] + extra
            rest = rest - extra
    return np.array([reach] + given)


def uneven_parts(own_key, number_of, total, reach, skew):
    if number_of == 2:
        one = jax.random.randint(own_key, (), max(1, total - reach), min(reach, total - 1) + 1)
        return jnp.stack([one, total - one])
    sizes = jnp.asarray(split_up(number_of, total, reach, skew), jnp.int32)
    couples = (number_of - 1) // 2
    donor, receiver = sizes[1:1 + 2 * couples:2], sizes[2:2 + 2 * couples:2]
    margin = jnp.minimum(donor - 1, reach - receiver)
    shifted = jax.random.randint(jax.random.fold_in(own_key, 1), (couples,), 0, 1 << 20) % (margin + 1)
    sizes = sizes.at[1:1 + 2 * couples:2].set(donor - shifted).at[2:2 + 2 * couples:2].set(receiver + shifted)
    return sizes[jax.random.permutation(jax.random.fold_in(own_key, 2), number_of)]


def centred(key, extent, deviation, limit, shards=(), kind=jnp.bfloat16):
    factor_of = level_of(key, extent, shards, -0.22, 0.18) if shards else 1.0
    values = jax.random.normal(key, extent, jnp.float32) * deviation * factor_of
    return jnp.minimum(jnp.maximum(values, -limit), limit).astype(kind)


def bell_draw_with(rng, shape, spread, bound, cuts, heavy, held_as=jnp.bfloat16):
    entries = spread * jax.random.normal(rng, shape, jnp.float32)
    if cuts:
        entries = entries * level_of(rng, shape, cuts, -0.22, 0.18)
    return jnp.clip(with_spikes(entries, jax.random.fold_in(rng, 3), *heavy), -bound, bound).astype(held_as)


def setup_inputs(seed: int = 0) -> dict:
    key_list = jax.random.split(jax.random.key(seed), 13)
    return {
        "inputs": centred(key_list[0], (MICRO, ROWS, ROW_LEN, D), 1.0, 6.0, ((1, 4), (2, 8))),
        "lengths": jax.vmap(lambda own: uneven_parts(own, SEQS, ROW_LEN, ROW_LEN * 3 // 4, 1))(jax.random.split(key_list[1], MICRO * ROWS)).reshape((MICRO, ROWS, SEQS)).astype(jnp.int32),
        "first_gain": jnp.clip(0.5 + 1.0 * jax.random.uniform(key_list[2], (D,), jnp.float32) ** level_of(key_list[2], (D,), ((0, 16),), -0.2, 0.2), 0.5, 1.5).astype(jnp.bfloat16),
        "second_gain": jnp.clip(0.5 + 1.0 * jax.random.uniform(key_list[3], (D,), jnp.float32) ** level_of(key_list[3], (D,), ((0, 16),), -0.2, 0.2), 0.5, 1.5).astype(jnp.bfloat16),
        "query_weight": centred(key_list[4], (D, HQ), D ** -0.5, 0.125, ((0, 16), (1, 2))),
        "key_weight": centred(key_list[5], (D, HQ), D ** -0.5, 0.125, ((0, 16), (1, 2))),
        "value_weight": centred(key_list[6], (D, VW), D ** -0.5, 0.125, ((0, 16), (1, 2))),
        "gate_weight": centred(key_list[7], (D, VW), D ** -0.5, 0.125, ((0, 16), (1, 2))),
        "out_weight": centred(key_list[8], (D, VW), (VW // 4) ** -0.5, 0.1875, ((0, 16), (1, 2))),
        "up_weight": centred(key_list[9], (D, FF), D ** -0.5, 0.125, ((0, 16), (1, 2))),
        "down_weight": centred(key_list[10], (D, FF), (FF // 2) ** -0.5, 0.125, ((0, 16), (1, 2))),
        "out_cotangent": bell_draw_with(key_list[11], (MICRO, ROWS, ROW_LEN, D), 1.0, 6.0, ((1, 4), (2, 8)), (2, 3, 8, 2.0)),
    }


PRECISION_MAX = lax.Precision.HIGHEST
EPSILON = 1e-05
GROUP_EPSILON = 1.0
XPOS_BASE = 512.0

@jax.custom_vjp
def low(v):
    return lax.optimization_barrier(v.astype(jnp.bfloat16)).astype(jnp.float32)

@jax.custom_vjp
def low_back(v):
    return v

def low_keep(v):
    return (low(v), None)

def low_pass(kept, grad):
    return (grad,)

def back_keep(v):
    return (v, None)

def back_low(kept, grad):
    return (low(grad),)
low.defvjp(low_keep, low_pass)
low_back.defvjp(back_keep, back_low)

def norm_rows(values, offset):
    centre = values - lax.optimization_barrier(jnp.mean(values, axis=-1, keepdims=True))
    inv_scale = lax.rsqrt(lax.optimization_barrier(jnp.mean(centre * centre, axis=-1, keepdims=True)) + offset)
    return (centre * inv_scale, inv_scale)

def layout(lengths_row, first_place, number):
    lengths_int = lengths_row.astype(jnp.int32)
    starts = (jnp.cumsum(lengths_int, dtype=jnp.int32).astype(jnp.int32) - lengths_int).astype(jnp.int32)
    places = (jnp.arange(number, dtype=jnp.int32) + jnp.int32(first_place)).astype(jnp.int32)
    is_after = places[:, None] >= starts[None, :]
    counted = lax.optimization_barrier(jnp.sum(is_after.astype(jnp.int32), axis=1, dtype=jnp.int32)).astype(jnp.int32)
    documents = (counted - jnp.int32(1)).astype(jnp.int32)
    zero_int = jnp.zeros((1, starts.shape[0]), dtype=jnp.int32)
    begins = lax.optimization_barrier(jnp.max(jnp.where(is_after, starts[None, :].astype(jnp.int32), zero_int), axis=1)).astype(jnp.int32)
    return (documents, (places - begins).astype(jnp.int32))

def rotation(places, sign_exp, head_width, float_type):
    half_width = head_width // 2
    pair_index = jnp.arange(half_width).astype(float_type)
    frequency = jnp.exp(pair_index * (-math.log(10000.0) / half_width))
    zeta_base = (2.0 * pair_index + 0.4 * head_width) / (1.4 * head_width)
    place_f = places.astype(float_type)[:, None]
    angle_t = place_f * frequency[None, :]
    factor = jnp.exp(place_f * (sign_exp / XPOS_BASE) * jnp.log(zeta_base)[None, :])
    return (jnp.cos(angle_t) * factor, jnp.sin(angle_t) * factor)

def rotate(values, cos_table, sin_table):
    half_width = values.shape[-1] // 2
    first_half = values[..., :half_width]
    second_half = values[..., half_width:]
    return jnp.concatenate([first_half * cos_table - second_half * sin_table, first_half * sin_table + second_half * cos_table], axis=-1)

def decay_parts(documents, previous, log_gamma):
    float_type = log_gamma.dtype
    tokens_n = documents.shape[0]
    steps_f = jnp.arange(tokens_n).astype(float_type)
    zero_f = jnp.zeros((), float_type)
    last_step = jnp.full((), tokens_n - 1).astype(float_type)
    whole_steps = jnp.full((), tokens_n).astype(float_type)
    distance = steps_f[:, None] - steps_f[None, :]
    same_doc = (documents[:, None] == documents[None, :]) & (distance >= zero_f)
    inner_decay = jnp.where(same_doc[None], jnp.exp(jnp.maximum(distance, zero_f)[None] * log_gamma[:, None, None]), zero_f)
    carried = jnp.where((documents == previous)[None, :], jnp.exp((steps_f + jnp.ones((), float_type))[None, :] * log_gamma[:, None]), zero_f)
    last_doc = documents[tokens_n - 1]
    leaving = jnp.where((documents == last_doc)[None, :], jnp.exp((last_step - steps_f)[None, :] * log_gamma[:, None]), zero_f)
    through = jnp.where(previous == last_doc, jnp.exp(whole_steps * log_gamma), zero_f)
    return (inner_decay, carried, leaving, through)

def dot_high(left_side, right_side):
    return jnp.dot(left_side, right_side, precision=PRECISION_MAX, preferred_element_type=left_side.dtype)

def dot_high_t(left_side, right_side):
    return lax.dot_general(left_side, right_side, (((1,), (1,)), ((), ())), precision=PRECISION_MAX, preferred_element_type=left_side.dtype)

def retention(queries, key_rows, value_rows, documents):
    float_type = queries.dtype
    blocks_n = ROW_LEN // BLOCK
    head_index = jnp.arange(HEADS).astype(float_type)
    log_gamma = jnp.log1p(-jnp.exp2(-5.0 - head_index)).astype(float_type)
    doc_blocks = documents.astype(jnp.int32).reshape(blocks_n, BLOCK)
    previous = jnp.concatenate([jnp.full((1,), -1, dtype=jnp.int32), doc_blocks[:-1, -1].astype(jnp.int32)]).astype(jnp.int32)

    def block_step(state_in, pieces):
        block_queries, block_keys, block_values, doc_block, prev_doc = pieces
        inner_decay, carried, leaving, through = decay_parts(doc_block, prev_doc, log_gamma)
        score_matrix = jnp.einsum('lba,qba->blq', block_queries, block_keys, precision=PRECISION_MAX)
        score_weights = low(low_back(score_matrix) * inner_decay)
        intra_part = jnp.einsum('hnm,mhe->nhe', score_weights, block_values, precision=PRECISION_MAX)
        queries_carried = block_queries * carried.T[:, :, None]
        outer_part = jnp.einsum('nhd,hde->nhe', queries_carried, state_in, precision=PRECISION_MAX)
        decayed_keys = block_keys * leaving.T[:, :, None]
        block_state = jnp.einsum('vfb,vfz->fbz', decayed_keys, block_values, precision=PRECISION_MAX)
        state_next = (through[:, None, None] * state_in + block_state).astype(float_type)
        return (state_next, (intra_part + outer_part).astype(float_type))
    initial = jnp.zeros((HEADS, QK, HV), dtype=float_type)
    pieces = (queries.reshape(blocks_n, BLOCK, HEADS, QK), key_rows.reshape(blocks_n, BLOCK, HEADS, QK), value_rows.reshape(blocks_n, BLOCK, HEADS, HV), doc_blocks, previous)
    unused, outputs = lax.scan(jax.checkpoint(block_step), initial, pieces)
    return outputs.reshape(ROW_LEN, HEADS, HV)

def row_forward(params, inputs_row, lengths_row):
    first_gain, second_gain, query_weight, key_weight, value_weight, gate_weight, out_weight, up_weight, down_weight = params
    float_type = inputs_row.dtype
    documents, places = layout(lengths_row, 0, ROW_LEN)
    cos_query, sin_query = rotation(places, 1.0, QK, float_type)
    cos_key, sin_key = rotation(places, -1.0, QK, float_type)
    normed_first, unused = norm_rows(inputs_row, EPSILON)
    hidden_first = low(normed_first * first_gain)
    query_pre = low_back(dot_high(hidden_first, query_weight)).reshape(ROW_LEN, HEADS, QK)
    key_pre = low_back(dot_high(hidden_first, key_weight)).reshape(ROW_LEN, HEADS, QK)
    queries = low(rotate(query_pre, cos_query[:, None, :], sin_query[:, None, :]))
    key_rows = low(rotate(key_pre, cos_key[:, None, :], sin_key[:, None, :]))
    value_rows = low(low_back(dot_high(hidden_first, value_weight))).reshape(ROW_LEN, HEADS, HV)
    gate_pre = low_back(dot_high(hidden_first, gate_weight))
    retained = low_back(retention(queries, key_rows, value_rows, documents))
    grouped, unused_group = norm_rows(retained, GROUP_EPSILON)
    mixed_rows = low(jax.nn.silu(gate_pre).reshape(ROW_LEN, HEADS, HV) * grouped).reshape(ROW_LEN, HEADS * HV)
    branch_attn = low_back(dot_high_t(mixed_rows, out_weight))
    middle = inputs_row + branch_attn
    normed_second, unused_second = norm_rows(middle, EPSILON)
    hidden_second = low(normed_second * second_gain)
    up_pre = low_back(dot_high(hidden_second, up_weight))
    activated = low(jax.nn.gelu(up_pre, approximate=False))
    branch_ffn = low_back(dot_high_t(activated, down_weight))
    return middle + branch_ffn

def reference(inputs, lengths, first_gain, second_gain, query_weight, key_weight, value_weight, gate_weight, out_weight, up_weight, down_weight, out_cotangent):
    params = tuple((member.astype(jnp.float32) for member in (first_gain, second_gain, query_weight, key_weight, value_weight, gate_weight, out_weight, up_weight, down_weight)))
    rows_all = MICRO * ROWS

    def row_step(totals, pieces):
        inputs_row, lengths_row, cotangent_row = pieces
        row_values = inputs_row.astype(jnp.float32)
        result, pullback = jax.vjp(lambda weights, values: row_forward(weights, values, lengths_row), params, row_values)
        grad_params, grad_row = pullback(cotangent_row.astype(result.dtype))
        totals = jax.tree.map(lambda running, adding: running + adding.astype(running.dtype), totals, grad_params)
        return (totals, (result.astype(jnp.bfloat16), grad_row.astype(jnp.bfloat16)))
    zero_totals = jax.tree.map(jnp.zeros_like, params)
    pieces = (inputs.reshape(rows_all, ROW_LEN, D), lengths.astype(jnp.int32).reshape(rows_all, SEQS), out_cotangent.reshape(rows_all, ROW_LEN, D))
    totals, (outputs, grads_in) = lax.scan(row_step, zero_totals, pieces)
    return (outputs.reshape(MICRO, ROWS, ROW_LEN, D), grads_in.reshape(MICRO, ROWS, ROW_LEN, D), totals[0], totals[1], totals[2], totals[3], totals[4], totals[5], totals[6], totals[7], totals[8])
```

```python
import math

import jax
import jax.numpy as jnp
from jax import lax
from jax.experimental import pallas as pl
from jax.experimental.pallas import tpu as pltpu
from jax.sharding import PartitionSpec as P

QK = 256
HV = 512
EPSILON = 1e-05
GROUP_EPSILON = 1.0
XPOS_BASE = 512.0


def norm_rows(values, offset):
    centre = values - jnp.mean(values, axis=-1, keepdims=True)
    inv_scale = lax.rsqrt(jnp.mean(centre * centre, axis=-1, keepdims=True) + offset)
    return (centre * inv_scale, inv_scale)


def norm_back(grad_terms, normed, inv_scale):
    grad_mean = jnp.mean(grad_terms, axis=-1, keepdims=True)
    cross_mean = jnp.mean(grad_terms * normed, axis=-1, keepdims=True)
    return inv_scale * (grad_terms - grad_mean - normed * cross_mean)


def layout(lengths_row, first_place, number):
    count = lengths_row.shape[0]
    before = jnp.arange(count)[None, :] < jnp.arange(count)[:, None]
    starts = jnp.sum(jnp.where(before, lengths_row[None, :], 0), axis=1, dtype=jnp.int32)
    places = first_place + jnp.arange(number, dtype=jnp.int32)
    is_after = places[:, None] >= starts[None, :]
    documents = jnp.sum(is_after.astype(jnp.int32), axis=1, dtype=jnp.int32) - 1
    begins = jnp.max(jnp.where(is_after, starts[None, :], 0), axis=1)
    return (documents, places - begins)


def rotation(places, sign_exp, head_width):
    half_width = head_width // 2
    pair_index = jnp.arange(half_width, dtype=jnp.float32)
    frequency = jnp.exp(pair_index * (-math.log(10000.0) / half_width))
    zeta_base = (2.0 * pair_index + 0.4 * head_width) / (1.4 * head_width)
    place_f = places.astype(jnp.float32)[:, None]
    angle_t = place_f * frequency[None, :]
    factor = jnp.exp(place_f * (sign_exp / XPOS_BASE) * jnp.log(zeta_base)[None, :])
    return (jnp.cos(angle_t) * factor, jnp.sin(angle_t) * factor)


def rotate(values, cos_table, sin_table):
    half_width = values.shape[-1] // 2
    first_half = values[..., :half_width]
    second_half = values[..., half_width:]
    return jnp.concatenate(
        [
            first_half * cos_table - second_half * sin_table,
            first_half * sin_table + second_half * cos_table,
        ],
        axis=-1,
    )


def rotate_back(grad_terms, cos_table, sin_table):
    return rotate(grad_terms, cos_table, -sin_table)


def decay_parts(documents, previous, log_gamma):
    tokens_n = documents.shape[0]
    steps_f = jnp.arange(tokens_n, dtype=jnp.float32)
    distance = steps_f[:, None] - steps_f[None, :]
    same_doc = (documents[:, None] == documents[None, :]) & (distance >= 0.0)
    inner_decay = jnp.where(
        same_doc[None], jnp.exp(jnp.maximum(distance, 0.0)[None] * log_gamma[:, None, None]), 0.0
    )
    carried = jnp.where(
        (documents == previous)[None, :],
        jnp.exp((steps_f + 1.0)[None, :] * log_gamma[:, None]),
        0.0,
    )
    last_doc = documents[tokens_n - 1]
    leaving = jnp.where(
        (documents == last_doc)[None, :],
        jnp.exp((tokens_n - 1.0 - steps_f)[None, :] * log_gamma[:, None]),
        0.0,
    )
    through = jnp.where(previous == last_doc, jnp.exp(tokens_n * log_gamma), 0.0)
    return (inner_decay, carried, leaving, through)


def gelu_exact(values):
    return jax.nn.gelu(values, approximate=False)


def matmul(left_side, right_side):
    return jnp.dot(left_side, right_side, preferred_element_type=jnp.float32)


def matmul_t(left_side, right_side):
    return lax.dot_general(
        left_side, right_side, (((1,), (1,)), ((), ())), preferred_element_type=jnp.float32
    )


def tmatmul(left_side, right_side):
    return lax.dot_general(
        left_side, right_side, (((0,), (0,)), ((), ())), preferred_element_type=jnp.float32
    )


def einsum(spec, left_side, right_side):
    return jnp.einsum(spec, left_side, right_side, preferred_element_type=jnp.float32)


def wide(values):
    return values.astype(jnp.float32)


def narrow(values):
    return values.astype(jnp.bfloat16)


class Plain:
    def __init__(self, tensor_heads):
        self.rows = 1
        self.heads = tensor_heads
        self.first_head = lax.axis_index("tensor") * tensor_heads

    def lengths(self, values):
        return values

    def gather_tokens(self, values):
        return lax.all_gather(values, "tensor", axis=0, tiled=True)

    def scatter_tokens(self, values):
        return wide(lax.psum_scatter(narrow(values), "tensor", scatter_dimension=0, tiled=True))

    def gather_weight(self, *shards):
        whole = [lax.all_gather(w, ("dp", "seq"), axis=0, tiled=True) for w in shards]
        return jnp.concatenate(whole, axis=1)

    def scatter_grad(self, grad, parts):
        grads = jnp.split(grad, parts, axis=1)
        return [
            wide(lax.psum_scatter(g, ("dp", "seq"), scatter_dimension=0, tiled=True))
            for g in grads
        ]


def chain(state, through, reverse):
    count, mine = lax.axis_size("seq"), lax.axis_index("seq")
    entering = jnp.zeros_like(state)
    for hop in range(1, count):
        leaving = state if hop == 1 else state + through[..., None, None] * entering
        pair = (count - hop, count - 1 - hop) if reverse else (hop - 1, hop)
        entering = entering + wide(lax.ppermute(narrow(leaving), "seq", [pair]))
    return entering


def plain_body(
    inputs,
    lengths,
    first_gain,
    second_gain,
    query_weight,
    key_weight,
    value_weight,
    gate_weight,
    out_weight,
    up_weight,
    down_weight,
    out_cotangent,
):
    micro = inputs.shape[0]
    shard_len = inputs.shape[2]
    block_len = shard_len * lax.axis_size("tensor")
    block_start = lax.axis_index("seq") * block_len
    tensor_heads = query_weight.shape[1] // QK
    plan = Plain(tensor_heads)
    rows, heads = plan.rows, plan.heads
    head_index = (plan.first_head + jnp.arange(heads, dtype=jnp.int32)).astype(jnp.float32)
    log_gamma = jnp.log1p(-jnp.exp2(-5.0 - head_index))
    half_width = QK // 2
    gain_one = wide(first_gain)[:, None]
    gain_two = wide(second_gain)[:, None]
    row_lengths = plan.lengths(lengths)

    def scaled(weight, gain):
        return narrow(wide(weight) * gain)

    weight_qk = plan.gather_weight(
        scaled(query_weight, gain_one), scaled(key_weight, gain_one)
    )
    weight_v = plan.gather_weight(scaled(value_weight, gain_one))
    weight_g = plan.gather_weight(scaled(gate_weight, gain_one))
    weight_o = plan.gather_weight(out_weight)
    weight_d = plan.gather_weight(down_weight)
    weight_u = plan.gather_weight(scaled(up_weight, gain_two))
    width_q = weight_qk.shape[1] // 2

    def row_plan(lengths_row):
        documents, places = layout(lengths_row, block_start, block_len)
        previous, unused = layout(lengths_row, block_start - 1, 1)
        return (documents, places, previous[0])

    def forward(inputs_mb, lengths_mb, cotangent_mb):
        tokens = rows * block_len
        documents, places, previous = jax.vmap(row_plan)(lengths_mb)
        flat_places = places.reshape(-1)
        tables = [
            table.reshape(rows, block_len, 1, half_width)
            for sign in (1.0, -1.0)
            for table in rotation(flat_places, sign, QK)
        ]
        decay = jax.vmap(decay_parts, in_axes=(0, 0, None))(documents, previous, log_gamma)
        inner_decay, carried, leaving, through = decay
        carried_t = jnp.swapaxes(carried, 1, 2)[..., None]
        leaving_t = jnp.swapaxes(leaving, 1, 2)[..., None]
        residual = wide(inputs_mb)
        normed_first, inv_first = norm_rows(residual, EPSILON)
        hidden_first = plan.gather_tokens(narrow(normed_first))
        qk_pre = matmul(hidden_first, weight_qk)
        query_pre = qk_pre[:, :width_q].reshape(rows, block_len, heads, QK)
        key_pre = qk_pre[:, width_q:].reshape(rows, block_len, heads, QK)
        value_rows = narrow(matmul(hidden_first, weight_v)).reshape(rows, block_len, heads, HV)
        gate_pre = matmul(hidden_first, weight_g)
        queries = narrow(rotate(query_pre, tables[0], tables[1]))
        key_rows = narrow(rotate(key_pre, tables[2], tables[3]))
        score_matrix = einsum("rnhd,rmhd->rhnm", queries, key_rows)
        score_weights = narrow(score_matrix * inner_decay)
        intra_part = einsum("rhnm,rmhe->rnhe", score_weights, value_rows)
        decayed_keys = narrow(wide(key_rows) * leaving_t)
        block_state = einsum("rmhd,rmhe->rhde", decayed_keys, value_rows)
        state_in = narrow(chain(block_state, through, False))
        queries_carried = narrow(wide(queries) * carried_t)
        retained = intra_part + einsum("rnhd,rhde->rnhe", queries_carried, state_in)
        grouped, inv_group = norm_rows(retained, GROUP_EPSILON)
        grouped_flat = grouped.reshape(tokens, -1)
        mixed_rows = narrow(jax.nn.silu(gate_pre) * grouped_flat)
        middle = residual + plan.scatter_tokens(matmul_t(mixed_rows, weight_o))
        normed_second, inv_second = norm_rows(middle, EPSILON)
        hidden_second = plan.gather_tokens(narrow(normed_second))
        up_pre = matmul(hidden_second, weight_u)
        activated = narrow(gelu_exact(up_pre))
        outputs = narrow(middle + plan.scatter_tokens(matmul_t(activated, weight_d)))

        grad_rows = plan.gather_tokens(cotangent_mb)
        grad_act = matmul(grad_rows, weight_d)
        grad_up_pre = narrow(jax.vjp(gelu_exact, up_pre)[1](grad_act)[0])
        back_second = plan.scatter_tokens(matmul_t(grad_up_pre, weight_u))
        grad_middle = wide(cotangent_mb) + norm_back(back_second, normed_second, inv_second)
        grad_attn = plan.gather_tokens(narrow(grad_middle))
        grad_mixed = matmul(grad_attn, weight_o)
        grad_gate_pre = narrow(
            jax.vjp(jax.nn.silu, gate_pre)[1](grad_mixed * grouped_flat)[0]
        )
        grad_grouped = (grad_mixed * jax.nn.silu(gate_pre)).reshape(
            rows, block_len, heads, HV
        )
        grad_retained = narrow(norm_back(grad_grouped, grouped, inv_group))
        grad_scores = einsum("rnhe,rmhe->rhnm", grad_retained, value_rows)
        score_grads = narrow(grad_scores * inner_decay)
        direct = einsum("rnhd,rnhe->rhde", queries_carried, grad_retained)
        state_out = narrow(chain(direct, through, True))
        grad_queries = einsum("rhnm,rmhd->rnhd", score_grads, key_rows) + carried_t * einsum(
            "rnhe,rhde->rnhd", grad_retained, state_in
        )
        grad_keys = einsum("rhnm,rnhd->rmhd", score_grads, queries) + leaving_t * einsum(
            "rmhe,rhde->rmhd", value_rows, state_out
        )
        grad_values = einsum("rhnm,rnhe->rmhe", score_weights, grad_retained) + einsum(
            "rmhd,rhde->rmhe", decayed_keys, state_out
        )
        grad_query_pre = narrow(rotate_back(grad_queries, tables[0], tables[1]))
        grad_key_pre = narrow(rotate_back(grad_keys, tables[2], tables[3]))
        grad_qk_pre = jnp.concatenate(
            [grad_query_pre.reshape(tokens, -1), grad_key_pre.reshape(tokens, -1)], axis=1
        )
        grad_value_pre = narrow(grad_values).reshape(tokens, -1)
        first_part = matmul_t(grad_qk_pre, weight_qk) + matmul_t(grad_value_pre, weight_v)
        first_part = first_part + matmul_t(grad_gate_pre, weight_g)
        back_first = plan.scatter_tokens(first_part)
        grad_inputs = narrow(grad_middle + norm_back(back_first, normed_first, inv_first))
        pieces = (
            (hidden_first, grad_qk_pre),
            (hidden_first, grad_value_pre),
            (hidden_first, grad_gate_pre),
            (grad_attn, mixed_rows),
            (hidden_second, grad_up_pre),
            (grad_rows, activated),
        )
        return (outputs, grad_inputs, pieces)

    done = [
        forward(inputs[i, :, :, :].reshape(shard_len * inputs.shape[1], -1), row_lengths[i],
                out_cotangent[i].reshape(shard_len * inputs.shape[1], -1))
        for i in range(micro)
    ]

    def weight_grad(k):
        total = sum(tmatmul(*done[i][2][k]) for i in range(micro))
        return narrow(total)

    grad_down = plan.scatter_grad(weight_grad(5), 1)[0]
    grad_up = plan.scatter_grad(weight_grad(4), 1)[0]
    grad_out = plan.scatter_grad(weight_grad(3), 1)[0]
    grad_gate = plan.scatter_grad(weight_grad(2), 1)[0]
    grad_value = plan.scatter_grad(weight_grad(1), 1)[0]
    grad_query, grad_key = plan.scatter_grad(weight_grad(0), 2)

    def along(weight, grad):
        return jnp.sum(wide(weight) * grad, axis=1)

    gain_sums = lax.psum(
        (
            along(query_weight, grad_query)
            + along(key_weight, grad_key)
            + along(value_weight, grad_value)
            + along(gate_weight, grad_gate),
            along(up_weight, grad_up),
        ),
        "tensor",
    )
    shape = inputs.shape
    return (
        jnp.stack([d[0] for d in done]).reshape(shape),
        jnp.stack([d[1] for d in done]).reshape(shape),
        gain_sums[0],
        gain_sums[1],
        grad_query * gain_one,
        grad_key * gain_one,
        grad_value * gain_one,
        grad_gate * gain_one,
        grad_out,
        grad_up * gain_two,
        grad_down,
    )


def swap(values, axis, bit):
    return lax.ppermute(values, axis, [(i, i ^ bit) for i in range(lax.axis_size(axis))])


def in_order(mine, other, index, axis):
    return jnp.where(
        index == 0, jnp.stack([mine, other], axis), jnp.stack([other, mine], axis)
    )


def pass_on(state, through, reverse, ties):
    count = lax.axis_size("seq")
    entering = []
    for hop in range(1, count):
        leaving = state
        if entering:
            before = tied(entering[-1], *ties.get(hop, ()))
            leaving = narrow(wide(state) + through[..., None, None] * wide(before))
        pair = (count - hop, count - 1 - hop) if reverse else (hop - 1, hop)
        entering.append(lax.ppermute(leaving, "seq", [pair]))
    return entering


def arrive(entering, *before):
    return sum(entering[:-1], tied(entering[-1], *before))


LANES = 128


def place_order(blocks):
    return [(up, block, side) for up in range(2) for block in range(blocks) for side in range(2)]


def group_of(place, upper, blocks):
    up, block, side = place
    start = (up ^ upper) if isinstance(upper, int) else lax.bitwise_xor(upper, up)
    return (start * 2 + side) * blocks + block


def load_groups(ref, upper, blocks):
    width = ref.shape[1] // (4 * blocks)
    parts = []
    for place in place_order(blocks):
        at = pl.multiple_of(group_of(place, upper, blocks) * width, LANES)
        parts.append(ref[:, pl.ds(at, width)])
    return jnp.concatenate(parts, axis=1)


def store_groups(ref, values, upper, blocks):
    width = ref.shape[1] // (4 * blocks)
    for i, place in enumerate(place_order(blocks)):
        at = pl.multiple_of(group_of(place, upper, blocks) * width, LANES)
        ref[:, pl.ds(at, width)] = values[:, i * width : (i + 1) * width]


VMEM_BYTES = 48 << 20


def tied(values, *others):
    return lax.optimization_barrier((values,) + others)[0]


def join(*columns):
    rows, widths = sum(p.shape[0] for p in columns[0]), [c[0].shape[1] for c in columns]
    parts = [p for c in columns for p in c]
    count = max(1, 4 // len(parts))

    def kernel(*refs):
        ins, (out, held, arrived, left) = refs[: len(parts)], refs[len(parts) :]
        pieces, number, across = [], 0, 0
        for width, column in zip(widths, columns):
            at = 0
            for _ in column:
                ref = ins[number]
                number += 1
                size = ref.shape[0] // count
                for k in range(count):
                    i, place = len(pieces), (pl.ds(at, size), pl.ds(across, width))
                    pieces.append(
                        (
                            pltpu.make_async_copy(
                                ref.at[pl.ds(k * size, size)], held.at[place], arrived.at[i]
                            ),
                            pltpu.make_async_copy(held.at[place], out.at[place], left.at[i]),
                        )
                    )
                    at += size
            across += width
        for copy_in, copy_out in pieces:
            copy_in.start()
        for copy_in, copy_out in pieces:
            copy_in.wait()
            copy_out.start()
        for copy_in, copy_out in pieces:
            copy_out.wait()

    number = len(parts) * count
    shape, dtype = (rows, sum(widths)), parts[0].dtype
    return pl.pallas_call(
        kernel,
        out_shape=jax.ShapeDtypeStruct(shape, dtype),
        in_specs=[pl.BlockSpec(memory_space=pl.ANY)] * len(parts),
        out_specs=pl.BlockSpec(memory_space=pl.ANY),
        scratch_shapes=[
            pltpu.VMEM(shape, dtype),
            pltpu.SemaphoreType.DMA((number,)),
            pltpu.SemaphoreType.DMA((number,)),
        ],
        compiler_params=pltpu.CompilerParams(vmem_limit_bytes=VMEM_BYTES),
    )(*parts)


def call(kernel, grid, in_specs, out_specs, out_shape, scalars, *operands, aliases=()):
    return pl.pallas_call(
        kernel,
        out_shape=out_shape,
        grid_spec=pltpu.PrefetchScalarGridSpec(
            num_scalar_prefetch=len(scalars),
            grid=grid,
            in_specs=in_specs,
            out_specs=out_specs,
        ),
        compiler_params=pltpu.CompilerParams(
            dimension_semantics=("arbitrary",) * len(grid), vmem_limit_bytes=VMEM_BYTES
        ),
        input_output_aliases={len(scalars) + i: o for i, o in aliases},
    )(*scalars, *operands)


ROWS_STEP = 64


def row_call(kernel, upper, tokens, operands, out_types, first=(), into=None):
    features = operands[0].shape[1]
    starts = list(first) + [0] * (len(operands) - len(first))

    def spec(start):
        return pl.BlockSpec(
            (ROWS_STEP, features), lambda i, *_: (i + start // ROWS_STEP, 0)
        )

    ins = [spec(start) for start in starts]
    outs = [spec(0)] * len(out_types)
    shapes = [jax.ShapeDtypeStruct((tokens, features), t) for t in out_types]
    aliases = ()
    if into is not None:
        whole, at, rows = into
        outs = [spec(at)]
        shapes = [jax.ShapeDtypeStruct((rows, features), out_types[0])]
        if whole is not None:
            plain = kernel

            def kernel(*refs):
                plain(*refs[:-2], refs[-1])

            aliases = ((len(operands), 0),)
            operands = tuple(operands) + (whole,)
            ins.append(pl.BlockSpec(memory_space=pl.ANY))
    return call(
        kernel, (tokens // ROWS_STEP,), ins, outs, shapes, [upper], *operands, aliases=aliases
    )


def enter_tokens(upper, blocks, tokens, start, inputs, cotangent):
    def kernel(up, x, c, normed, x_out, c_out):
        values = load_groups(x, up[0], blocks)
        x_out[...] = values
        c_out[...] = load_groups(c, up[0], blocks)
        normed[...] = narrow(norm_rows(wide(values), EPSILON)[0])

    return row_call(
        kernel, upper, tokens, (inputs, cotangent), (jnp.bfloat16,) * 3, (start, start)
    )


def total(parts):
    return sum(wide(p[...]) for p in parts)


def middle_tokens(upper, inputs, parts):
    def kernel(up, x, a, b, c, middle, normed):
        values = wide(x[...]) + total((a, b, c))
        middle[...] = values
        normed[...] = narrow(norm_rows(values, EPSILON)[0])

    return row_call(
        kernel, upper, inputs.shape[0], (inputs,) + parts, (jnp.float32, jnp.bfloat16)
    )


def output_tokens(upper, blocks, middle, parts, into):
    def kernel(up, m, a, b, c, out):
        store_groups(out, narrow(m[...] + total((a, b, c))), up[0], blocks)

    return row_call(
        kernel, upper, middle.shape[0], (middle,) + parts, (jnp.bfloat16,), into=into
    )[0]


def back_middle(upper, middle, cotangent, parts):
    def kernel(up, m, g, a, b, c, grad, grad_narrow):
        normed, inv = norm_rows(m[...], EPSILON)
        values = wide(g[...]) + norm_back(total((a, b, c)), normed, inv)
        grad[...] = values
        grad_narrow[...] = narrow(values)

    return row_call(
        kernel,
        upper,
        middle.shape[0],
        (middle, cotangent) + parts,
        (jnp.float32, jnp.bfloat16),
    )


def back_inputs(upper, blocks, inputs, grad_middle, parts, into):
    def kernel(up, x, g, a, b, c, out):
        normed, inv = norm_rows(wide(x[...]), EPSILON)
        values = g[...] + norm_back(total((a, b, c)), normed, inv)
        store_groups(out, narrow(values), up[0], blocks)

    return row_call(
        kernel,
        upper,
        inputs.shape[0],
        (inputs, grad_middle) + parts,
        (jnp.bfloat16,),
        into=into,
    )[0]


def dot(left, right, left_dim, right_dim):
    return lax.dot_general(
        left, right, (((left_dim,), (right_dim,)), ((), ())), preferred_element_type=jnp.float32
    )


class Retention:
    def __init__(self, plan, log_gamma, core, documents, previous, tables):
        rows, length = documents.shape
        self.rows, self.heads, self.length = rows, plan.heads, length
        self.q_wide, self.v_wide = plan.heads * QK, plan.heads * HV
        last = documents[:, -1]
        self.scalars = [
            jnp.concatenate([core[None], previous, last]).astype(jnp.int32),
            log_gamma,
        ]
        self.documents = [documents[:, :, None], documents[:, None, :]]
        self.tables = tables

    def token_spec(self, width):
        return pl.BlockSpec(
            (2, None, self.length // 2, width), lambda r, *_: (0, r, 0, 0)
        )

    def head_spec(self, *shape):
        return pl.BlockSpec(
            (None, self.heads) + shape, lambda r, *_: (r, 0) + (0,) * len(shape)
        )

    def row_spec(self, *shape):
        return pl.BlockSpec((None,) + shape, lambda r, *_: (r,) + (0,) * len(shape))

    def token_type(self, width, dtype=jnp.bfloat16):
        return jax.ShapeDtypeStruct((2, self.rows, self.length // 2, width), dtype)

    def head_type(self, *shape, dtype=jnp.bfloat16):
        return jax.ShapeDtypeStruct((self.rows, self.heads) + shape, dtype)

    def tokens(self, values):
        return values.reshape(2, self.rows, self.length // 2, -1)

    def document_specs(self):
        return [self.row_spec(self.length, 1), self.row_spec(1, self.length)]

    def table_specs(self):
        return [self.row_spec(self.length, QK // 2)] * 2

    def run(self, kernel, in_specs, out, operands):
        return call(
            kernel,
            (self.rows,),
            in_specs,
            [spec for spec, shape in out],
            [shape for spec, shape in out],
            self.scalars,
            *operands,
        )

    def load(self, ref, core, at, width):
        return jnp.concatenate(
            [ref[core, :, at : at + width], ref[1 - core, :, at : at + width]], axis=0
        )

    def store(self, ref, core, at, values):
        half, width = self.length // 2, values.shape[1]
        ref[core, :, at : at + width] = values[:half]
        ref[1 - core, :, at : at + width] = values[half:]

    def carried(self, numbers, log_gamma, docs, row, head):
        steps = wide(lax.broadcasted_iota(jnp.int32, (self.length, 1), 0))
        kept = jnp.exp((steps + 1.0) * log_gamma[head])
        return jnp.where(docs[...] == numbers[1 + row], kept, 0.0)

    def leaving(self, numbers, log_gamma, docs, row, head):
        steps = wide(lax.broadcasted_iota(jnp.int32, (self.length, 1), 0))
        kept = jnp.exp((self.length - 1.0 - steps) * log_gamma[head])
        return jnp.where(docs[...] == numbers[1 + self.rows + row], kept, 0.0)

    def inner(self, log_gamma, docs, docs_t, head):
        shape = (self.length, self.length)
        distance = wide(
            lax.broadcasted_iota(jnp.int32, shape, 0) - lax.broadcasted_iota(jnp.int32, shape, 1)
        )
        kept = jnp.exp(jnp.maximum(distance, 0.0) * log_gamma[head])
        return jnp.where((docs[...] == docs_t[...]) & (distance >= 0.0), kept, 0.0)

    def retained(self, numbers, log_gamma, docs, docs_t, row, head, query, key, value, state):
        inner = self.inner(log_gamma, docs, docs_t, head)
        weights = narrow(dot(query, key, 1, 1) * inner)
        carried = self.carried(numbers, log_gamma, docs, row, head)
        values = dot(weights, value, 1, 0) + carried * dot(query, state, 1, 0)
        grouped, inv = norm_rows(values, GROUP_EPSILON)
        return inner, weights, carried, grouped, inv

    def keys(self, kv_pre):
        def kernel(numbers, log_gamma, kv, docs, docs_t, cos, sin, keys, values, state):
            row, core = pl.program_id(0), numbers[0]
            for head in range(self.heads):
                key = self.load(kv, core, head * QK, QK)
                key = narrow(rotate(key, cos[...], sin[...]))
                value = narrow(self.load(kv, core, self.q_wide + head * HV, HV))
                leaving = self.leaving(numbers, log_gamma, docs, row, head)
                keys[head] = key
                values[head] = value
                state[head] = narrow(dot(narrow(wide(key) * leaving), value, 0, 0))

        n = self.length
        return self.run(
            kernel,
            [self.token_spec(self.q_wide + self.v_wide)] + self.document_specs() + self.table_specs(),
            [
                (self.head_spec(n, QK), self.head_type(n, QK)),
                (self.head_spec(n, HV), self.head_type(n, HV)),
                (self.head_spec(QK, HV), self.head_type(QK, HV)),
            ],
            [self.tokens(kv_pre)] + self.documents + self.tables[2:],
        )

    def mix(self, qg_pre, keys, values, state_in):
        def kernel(
            numbers, log_gamma, qg, key_ref, value_ref, state_ref, docs, docs_t, cos, sin,
            queries, mixed,
        ):
            row, core = pl.program_id(0), numbers[0]
            for head in range(self.heads):
                query = self.load(qg, core, head * QK, QK)
                query = narrow(rotate(query, cos[...], sin[...]))
                queries[head] = query
                grouped = self.retained(
                    numbers, log_gamma, docs, docs_t, row, head,
                    query, key_ref[head], value_ref[head], state_ref[head],
                )[3]
                gate = self.load(qg, core, self.q_wide + head * HV, HV)
                out = narrow(gate * jax.nn.sigmoid(gate) * grouped)
                self.store(mixed, core, head * HV, out)

        n = self.length
        queries, mixed = self.run(
            kernel,
            [
                self.token_spec(self.q_wide + self.v_wide),
                self.head_spec(n, QK),
                self.head_spec(n, HV),
                self.head_spec(QK, HV),
            ]
            + self.document_specs()
            + self.table_specs(),
            [
                (self.head_spec(n, QK), self.head_type(n, QK)),
                (self.token_spec(self.v_wide), self.token_type(self.v_wide)),
            ],
            [self.tokens(qg_pre), keys, values, state_in] + self.documents + self.tables[:2],
        )
        return queries, mixed.reshape(-1, self.v_wide)

    def back(self, qg_pre, grad_mixed, queries, keys, values, state_in):
        def kernel(
            numbers, log_gamma, qg, grad_ref, query_ref, key_ref, value_ref, state_ref,
            docs, docs_t, cos, sin, grad_qg, direct, grad_keys, grad_values,
        ):
            row, core = pl.program_id(0), numbers[0]
            for head in range(self.heads):
                query, key, value = query_ref[head], key_ref[head], value_ref[head]
                state = state_ref[head]
                inner, weights, carried, grouped, inv = self.retained(
                    numbers, log_gamma, docs, docs_t, row, head, query, key, value, state
                )
                gate = self.load(qg, core, self.q_wide + head * HV, HV)
                grad = self.load(grad_ref, core, head * HV, HV)
                sigmoid = jax.nn.sigmoid(gate)
                grad_gate = grad * grouped * (sigmoid * (1.0 + gate * (1.0 - sigmoid)))
                self.store(grad_qg, core, self.q_wide + head * HV, narrow(grad_gate))
                grad_retained = narrow(norm_back(grad * (gate * sigmoid), grouped, inv))
                score_grads = narrow(dot(grad_retained, value, 1, 1) * inner)
                direct[head] = narrow(
                    dot(narrow(wide(query) * carried), grad_retained, 0, 0)
                )
                grad_query = dot(score_grads, key, 1, 0) + carried * dot(
                    grad_retained, state, 1, 1
                )
                grad_query = rotate_back(grad_query, cos[...], sin[...])
                self.store(grad_qg, core, head * QK, narrow(grad_query))
                grad_keys[head] = dot(score_grads, query, 0, 0)
                grad_values[head] = dot(weights, grad_retained, 0, 0)

        n = self.length
        wide_all = self.q_wide + self.v_wide
        return self.run(
            kernel,
            [
                self.token_spec(wide_all),
                self.token_spec(self.v_wide),
                self.head_spec(n, QK),
                self.head_spec(n, QK),
                self.head_spec(n, HV),
                self.head_spec(QK, HV),
            ]
            + self.document_specs()
            + self.table_specs(),
            [
                (self.token_spec(wide_all), self.token_type(wide_all)),
                (self.head_spec(QK, HV), self.head_type(QK, HV)),
                (self.head_spec(n, QK), self.head_type(n, QK, dtype=jnp.float32)),
                (self.head_spec(n, HV), self.head_type(n, HV, dtype=jnp.float32)),
            ],
            [self.tokens(qg_pre), self.tokens(grad_mixed), queries, keys, values, state_in]
            + self.documents
            + self.tables[:2],
        )

    def back_keys(self, keys, values, state_out, grad_keys, grad_values):
        def kernel(
            numbers, log_gamma, key_ref, value_ref, state_ref, key_part, value_part,
            docs, docs_t, cos, sin, grad_kv,
        ):
            row, core = pl.program_id(0), numbers[0]
            for head in range(self.heads):
                leaving = self.leaving(numbers, log_gamma, docs, row, head)
                state = state_ref[head]
                grad_key = key_part[head] + leaving * dot(value_ref[head], state, 1, 1)
                grad_key = rotate_back(grad_key, cos[...], sin[...])
                self.store(grad_kv, core, head * QK, narrow(grad_key))
                grad_value = value_part[head] + leaving * dot(key_ref[head], state, 1, 0)
                self.store(grad_kv, core, self.q_wide + head * HV, narrow(grad_value))

        n = self.length
        wide_all = self.q_wide + self.v_wide
        return self.run(
            kernel,
            [
                self.head_spec(n, QK),
                self.head_spec(n, HV),
                self.head_spec(QK, HV),
                self.head_spec(n, QK),
                self.head_spec(n, HV),
            ]
            + self.document_specs()
            + self.table_specs(),
            [(self.token_spec(wide_all), self.token_type(wide_all))],
            [keys, values, state_out, grad_keys, grad_values] + self.documents + self.tables[2:],
        )[0].reshape(-1, wide_all)


class Paired:
    def __init__(self, tensor_heads):
        self.rows = 2
        self.heads = tensor_heads // 2
        self.side = lax.axis_index("dp") % 2
        self.upper = (lax.axis_index("dp") // 2).astype(jnp.int32)
        self.core = lax.axis_index("tensor")
        self.blocks = lax.axis_size("seq")
        self.first_head = self.core * tensor_heads + self.side * self.heads

    def gather_tokens(self, values, *before):
        across = tied(swap(values, "dp", 1), *before)
        own = (values, swap(values, "tensor", 1))
        return join((own[0], across, own[1], swap(across, "tensor", 1)))

    def scatter_tokens(self, product):
        away = swap(product(1), "tensor", 1)
        here = product(0)
        half = here.shape[0] // 2
        across = narrow(wide(here[half:]) + wide(away[half:]))
        return (here[:half], away[:half], swap(across, "dp", 1)), here, across

    def halves(self, shard, which):
        width = shard.shape[1] // 2
        return lax.dynamic_slice_in_dim(shard, which * width, width, 1)

    def swap_weight(self, shards, *before):
        here = jnp.concatenate([self.halves(w, self.side) for w in shards], axis=1)
        away = jnp.concatenate([self.halves(w, 1 - self.side) for w in shards], axis=1)
        return here, swap(tied(away, *before), "dp", 1)

    def pair_weight(self, here, across):
        return in_order(here, across, self.side, 0).reshape(-1, here.shape[1])

    def across_grad(self, away, here, *before):
        return narrow(wide(tied(here, *before)) + wide(swap(away, "dp", 2)))

    def scatter_grad(self, quads, widths):
        mine, other = [], []
        for quad in quads:
            two = lax.psum_scatter(quad, "seq", scatter_dimension=0, tiled=True)
            two = two.reshape(2, -1, quad.shape[1])
            away = lax.dynamic_index_in_dim(two, 1 - self.side, 0, False)
            mine.append(wide(lax.dynamic_index_in_dim(two, self.side, 0, False)))
            other.append(wide(swap(away, "dp", 1)))
        mine, other = jnp.concatenate(mine, axis=1), jnp.concatenate(other, axis=1)
        out, at = [], 0
        for width in widths:
            part = in_order(mine[:, at : at + width], other[:, at : at + width], self.side, 1)
            out.append(part.reshape(mine.shape[0], -1))
            at += width
        return out


def paired_body(
    inputs,
    lengths,
    first_gain,
    second_gain,
    query_weight,
    key_weight,
    value_weight,
    gate_weight,
    out_weight,
    up_weight,
    down_weight,
    out_cotangent,
):
    micro = inputs.shape[0]
    shard_len, features = inputs.shape[2:]
    block_len = shard_len * 2
    block_start = lax.axis_index("seq") * block_len
    plan = Paired(query_weight.shape[1] // QK)
    rows, heads, blocks = plan.rows, plan.heads, plan.blocks
    upper = plan.upper[None]
    head_index = (plan.first_head + jnp.arange(heads, dtype=jnp.int32)).astype(jnp.float32)
    log_gamma = jnp.log1p(-jnp.exp2(-5.0 - head_index))
    gain_one = wide(first_gain)[:, None]
    gain_two = wide(second_gain)[:, None]
    row_lengths = jnp.concatenate([lengths, swap(lengths, "dp", 1)], axis=1)

    def scaled(weight, gain):
        return narrow(wide(weight) * gain)

    flat = (micro * shard_len, features)
    units = [
        (scaled(key_weight, gain_one), scaled(value_weight, gain_one)),
        (scaled(query_weight, gain_one), scaled(gate_weight, gain_one)),
        (out_weight,),
        (down_weight,),
        (scaled(up_weight, gain_two),),
    ]
    here, across = plan.swap_weight(units[0])
    entered = [
        enter_tokens(
            upper,
            blocks,
            shard_len,
            i * shard_len,
            inputs.reshape(flat),
            out_cotangent.reshape(flat),
        )
        for i in range(micro)
    ]
    across = tied(across, *[e[0] for e in entered])

    def spread(two, *before):
        return lax.all_gather(tied(two, *before), "seq", axis=0, tiled=True)

    two_kv = plan.pair_weight(here, across)
    cut = two_kv.shape[1] // 2
    quads_kv = [spread(two_kv[:, :cut]), spread(two_kv[:, cut:])]
    hidden_first = [plan.gather_tokens(e[0]) for e in entered]
    two_qg = plan.pair_weight(*plan.swap_weight(units[1], two_kv))
    quad_qg = spread(two_qg)
    two_o = plan.pair_weight(*plan.swap_weight(units[2], two_qg))
    quad_o = spread(two_o)
    quads_kv[0] = quad_kv = tied(quads_kv[0], two_o)
    others_kv = [swap(quad_kv, "dp", 2)]
    others_kv.append(swap(tied(quads_kv[1], *others_kv), "dp", 2))
    two_d = plan.pair_weight(*plan.swap_weight(units[3], quad_kv))
    two_u = plan.pair_weight(*plan.swap_weight(units[4], two_d))
    grad_rows = [plan.gather_tokens(tied(e[2], quad_kv)) for e in entered]
    others_kv[1] = tied(others_kv[1], two_u)
    other_qg = swap(tied(quad_qg, others_kv[1]), "dp", 2)
    other_o = swap(tied(quad_o, other_qg), "dp", 2)
    weight_kv = join(*zip(quads_kv, others_kv))
    weight_qg = join((quad_qg, other_qg))
    weight_o = join((quad_o, other_o))

    def row_plan(lengths_row):
        documents, places = layout(lengths_row, block_start, block_len)
        previous, unused = layout(lengths_row, block_start - 1, 1)
        return (documents, places, previous[0])

    kernels, throughs = [], []
    for i in range(micro):
        documents, places, previous = jax.vmap(row_plan)(row_lengths[i])
        tables = [
            table.reshape(rows, block_len, QK // 2)
            for sign in (1.0, -1.0)
            for table in rotation(places.reshape(-1), sign, QK)
        ]
        kernels.append(Retention(plan, log_gamma, plan.core, documents, previous, tables))
        throughs.append(
            jnp.where(
                (previous == documents[:, -1])[:, None], jnp.exp(block_len * log_gamma)[None], 0.0
            )
        )

    each = range(micro)
    half = rows * shard_len

    def rows_of(values, away):
        return values[half:] if away else values[:half]

    def product_t(values, weight):
        return lambda away: narrow(matmul_t(rows_of(values, away), weight))

    def products(left, right, columns=slice(None)):
        middle = features // 2
        return [
            narrow(sum(tmatmul(left[i][:, rows_cut], right[i][:, columns]) for i in each))
            for rows_cut in (slice(middle, None), slice(None, middle))
        ]

    def first_product(i):
        def run(away):
            part = matmul_t(rows_of(first_qg[i], away), weight_qg)
            return narrow(part + matmul_t(rows_of(first_kv[i], away), weight_kv))

        return run

    kv_pre = [matmul(hidden_first[i], weight_kv) for i in each]
    kvs = [kernels[0].keys(kv_pre[0])]
    kv_pre[1] = tied(kv_pre[1], *grad_rows, kvs[0][2])
    kvs.append(kernels[1].keys(kv_pre[1]))
    qg_pre = [matmul(hidden_first[i], weight_qg) for i in each]
    ties = [{}, {2: (other_qg,), 3: (other_o,)}]
    states = [pass_on(kvs[i][2], throughs[i], False, ties[i]) for i in each]
    quad_d = spread(two_d)
    quad_u = spread(two_u, states[0][1])
    other_d = swap(tied(quad_d, other_o), "dp", 2)
    other_u = swap(tied(quad_u, other_d), "dp", 2)
    weight_d = join((quad_d, other_d))
    weight_u = join((quad_u, other_u))
    mixes, attn, state_in = [], [], []
    before = (*qg_pre, other_o)
    for i in each:
        state_in.append(arrive(states[i], *before))
        mixes.append(kernels[i].mix(qg_pre[i], kvs[i][0], kvs[i][1], state_in[i]))
        parts, here, across = plan.scatter_tokens(product_t(mixes[i][1], weight_o))
        attn.append(parts)
        before = (here,)
    residual = [e[1] for e in entered]
    grad_act = [matmul(grad_rows[i], weight_d) for i in each]
    residual[0] = tied(residual[0], other_d)
    residual[1] = tied(residual[1], *grad_act)
    middles = [middle_tokens(upper, residual[i], attn[i]) for i in each]
    hidden_second = [plan.gather_tokens(middles[i][1]) for i in each]
    up_pre = [matmul(hidden_second[i], weight_u) for i in each]
    activated = [narrow(gelu_exact(up_pre[i])) for i in each]
    grad_up_pre = [
        narrow(jax.vjp(gelu_exact, up_pre[i])[1](grad_act[i])[0]) for i in each
    ]
    second, before = [], ()
    for i in each:
        product = product_t(tied(grad_up_pre[i], *before), weight_u)
        parts, here, across = plan.scatter_tokens(product)
        second.append(parts)
        before = (across,)
    down_products = products(grad_rows, [tied(a, here) for a in activated])
    middles[0] = (tied(middles[0][0], across), middles[0][1])
    grad_middle = [
        back_middle(upper, middles[i][0], entered[i][2], second[i]) for i in each
    ]
    up_products = products(
        hidden_second, [tied(g, grad_middle[0][1]) for g in grad_up_pre]
    )
    quad_down = plan.across_grad(*down_products, grad_middle[0][1])
    quad_up = plan.across_grad(*up_products, grad_middle[1][1])
    grad_attn, backs = [], []
    before = ()
    for i in each:
        grad_attn.append(plan.gather_tokens(grad_middle[i][1], *before))
        source = tied(grad_attn[i], grad_middle[1][1])
        grad_mixed = tied(matmul(source, weight_o), *((quad_down, quad_up) if i else ()))
        kv = kvs[i]
        backs.append(
            kernels[i].back(qg_pre[i], grad_mixed, mixes[i][0], kv[0], kv[1], state_in[i])
        )
        before = (backs[i][1],)
    after_back = backs[-1][1]
    grad_qg_pre = [b[0].reshape(-1, b[0].shape[-1]) for b in backs]
    out_products = products(grad_attn, [tied(m[1], after_back) for m in mixes])
    qg_products = products(hidden_first, [tied(g, out_products[1]) for g in grad_qg_pre])
    late = [tied(a, after_back) for a in activated]
    ffn = [plan.scatter_tokens(product_t(late[i], weight_d)) for i in each]
    states = [
        pass_on(backs[i][1], throughs[i], True, {2: (out_products[i],), 3: (qg_products[i],)})
        for i in each
    ]
    state_out = [arrive(states[i], ffn[0][1], ffn[1][1]) for i in each]
    outputs = grad_inputs = None
    for i in each:
        into = (outputs, i * shard_len, flat[0])
        outputs = output_tokens(upper, blocks, middles[i][0], ffn[i][0], into)
    grad_kv_pre = [
        kernels[i].back_keys(kvs[i][0], kvs[i][1], state_out[i], backs[i][2], backs[i][3])
        for i in each
    ]
    cut = grad_kv_pre[0].shape[1] // 2
    kv_products = [
        products(hidden_first, grad_kv_pre, columns)
        for columns in (slice(None, cut), slice(cut, None))
    ]
    first_qg = [tied(g, kv_products[1][1]) for g in grad_qg_pre]
    first_kv = [tied(g, kv_products[1][1]) for g in grad_kv_pre]
    first = [plan.scatter_tokens(first_product(i))[0] for i in each]
    for i in each:
        into = (grad_inputs, i * shard_len, flat[0])
        grad_inputs = back_inputs(
            upper, blocks, entered[i][1], grad_middle[i][0], first[i], into
        )

    width_q, width_v = heads * QK, heads * HV
    width_f = up_weight.shape[1] // 2
    grad_down = plan.scatter_grad([quad_down], [width_f])[0]
    grad_up = plan.scatter_grad([quad_up], [width_f])[0]
    quad_out = plan.across_grad(*out_products, state_out[0])
    grad_out = plan.scatter_grad([quad_out], [width_v])[0]
    quad_qg = plan.across_grad(*qg_products, *state_out)
    grad_query, grad_gate = plan.scatter_grad([quad_qg], [width_q, width_v])
    quads_kv = [plan.across_grad(*p) for p in kv_products]
    grad_key, grad_value = plan.scatter_grad(quads_kv, [width_q, width_v])

    def along(weight, grad):
        return jnp.sum(wide(weight) * grad, axis=1)

    gain_sums = lax.psum(
        (
            along(query_weight, grad_query)
            + along(key_weight, grad_key)
            + along(value_weight, grad_value)
            + along(gate_weight, grad_gate),
            along(up_weight, grad_up),
        ),
        "tensor",
    )
    return (
        outputs.reshape(inputs.shape),
        grad_inputs.reshape(inputs.shape),
        gain_sums[0],
        gain_sums[1],
        grad_query * gain_one,
        grad_key * gain_one,
        grad_value * gain_one,
        grad_gate * gain_one,
        grad_out,
        grad_up * gain_two,
        grad_down,
    )


def body(inputs, lengths, first_gain, second_gain, query_weight, *rest):
    paired = (
        lax.axis_size("dp") == 4
        and lax.axis_size("tensor") == 2
        and inputs.shape[1] == 1
        and query_weight.shape[1] % (2 * QK) == 0
        and inputs.shape[3] % (4 * lax.axis_size("seq") * LANES) == 0
        and inputs.shape[2] % ROWS_STEP == 0
    )
    run = paired_body if paired else plain_body
    return run(inputs, lengths, first_gain, second_gain, query_weight, *rest)


def solution(mesh):
    tokens = P(None, "dp", ("seq", "tensor"), None)
    vector = P(("dp", "seq"))
    matrix = P(("dp", "seq"), "tensor")
    return jax.shard_map(
        body,
        mesh=mesh,
        in_specs=(tokens, P(None, "dp", None), vector, vector) + (matrix,) * 7 + (tokens,),
        out_specs=(tokens, tokens, vector, vector) + (matrix,) * 7,
        check_vma=False,
    )
```

```python
import math

import jax
import jax.numpy as jnp
from jax import lax
from jax.experimental import pallas as pl
from jax.experimental.pallas import tpu as pltpu
from jax.sharding import PartitionSpec as P

QK = 256
HV = 512
EPSILON = 1e-05
GROUP_EPSILON = 1.0
XPOS_BASE = 512.0


def norm_rows(values, offset):
    centre = values - jnp.mean(values, axis=-1, keepdims=True)
    inv_scale = lax.rsqrt(jnp.mean(centre * centre, axis=-1, keepdims=True) + offset)
    return (centre * inv_scale, inv_scale)


def norm_back(grad_terms, normed, inv_scale):
    grad_mean = jnp.mean(grad_terms, axis=-1, keepdims=True)
    cross_mean = jnp.mean(grad_terms * normed, axis=-1, keepdims=True)
    return inv_scale * (grad_terms - grad_mean - normed * cross_mean)


def layout(lengths_row, first_place, number):
    count = lengths_row.shape[0]
    before = jnp.arange(count)[None, :] < jnp.arange(count)[:, None]
    starts = jnp.sum(jnp.where(before, lengths_row[None, :], 0), axis=1, dtype=jnp.int32)
    places = first_place + jnp.arange(number, dtype=jnp.int32)
    is_after = places[:, None] >= starts[None, :]
    documents = jnp.sum(is_after.astype(jnp.int32), axis=1, dtype=jnp.int32) - 1
    begins = jnp.max(jnp.where(is_after, starts[None, :], 0), axis=1)
    return (documents, places - begins)


def rotation(places, sign_exp, head_width):
    half_width = head_width // 2
    pair_index = jnp.arange(half_width, dtype=jnp.float32)
    frequency = jnp.exp(pair_index * (-math.log(10000.0) / half_width))
    zeta_base = (2.0 * pair_index + 0.4 * head_width) / (1.4 * head_width)
    place_f = places.astype(jnp.float32)[:, None]
    angle_t = place_f * frequency[None, :]
    factor = jnp.exp(place_f * (sign_exp / XPOS_BASE) * jnp.log(zeta_base)[None, :])
    return (jnp.cos(angle_t) * factor, jnp.sin(angle_t) * factor)


def rotate(values, cos_table, sin_table):
    half_width = values.shape[-1] // 2
    first_half = values[..., :half_width]
    second_half = values[..., half_width:]
    return jnp.concatenate(
        [
            first_half * cos_table - second_half * sin_table,
            first_half * sin_table + second_half * cos_table,
        ],
        axis=-1,
    )


def rotate_back(grad_terms, cos_table, sin_table):
    return rotate(grad_terms, cos_table, -sin_table)


def decay_parts(documents, previous, log_gamma):
    tokens_n = documents.shape[0]
    steps_f = jnp.arange(tokens_n, dtype=jnp.float32)
    distance = steps_f[:, None] - steps_f[None, :]
    same_doc = (documents[:, None] == documents[None, :]) & (distance >= 0.0)
    inner_decay = jnp.where(
        same_doc[None], jnp.exp(jnp.maximum(distance, 0.0)[None] * log_gamma[:, None, None]), 0.0
    )
    carried = jnp.where(
        (documents == previous)[None, :],
        jnp.exp((steps_f + 1.0)[None, :] * log_gamma[:, None]),
        0.0,
    )
    last_doc = documents[tokens_n - 1]
    leaving = jnp.where(
        (documents == last_doc)[None, :],
        jnp.exp((tokens_n - 1.0 - steps_f)[None, :] * log_gamma[:, None]),
        0.0,
    )
    through = jnp.where(previous == last_doc, jnp.exp(tokens_n * log_gamma), 0.0)
    return (inner_decay, carried, leaving, through)


def gelu_exact(values):
    return jax.nn.gelu(values, approximate=False)


def matmul(left_side, right_side):
    return jnp.dot(left_side, right_side, preferred_element_type=jnp.float32)


def matmul_t(left_side, right_side):
    return lax.dot_general(
        left_side, right_side, (((1,), (1,)), ((), ())), preferred_element_type=jnp.float32
    )


def tmatmul(left_side, right_side):
    return lax.dot_general(
        left_side, right_side, (((0,), (0,)), ((), ())), preferred_element_type=jnp.float32
    )


def einsum(spec, left_side, right_side):
    return jnp.einsum(spec, left_side, right_side, preferred_element_type=jnp.float32)


def wide(values):
    return values.astype(jnp.float32)


def narrow(values):
    return values.astype(jnp.bfloat16)


class Plain:
    def __init__(self, tensor_heads):
        self.rows = 1
        self.heads = tensor_heads
        self.first_head = lax.axis_index("tensor") * tensor_heads

    def lengths(self, values):
        return values

    def gather_tokens(self, values):
        return lax.all_gather(values, "tensor", axis=0, tiled=True)

    def scatter_tokens(self, values):
        return wide(lax.psum_scatter(narrow(values), "tensor", scatter_dimension=0, tiled=True))

    def gather_weight(self, *shards):
        whole = [lax.all_gather(w, ("dp", "seq"), axis=0, tiled=True) for w in shards]
        return jnp.concatenate(whole, axis=1)

    def scatter_grad(self, grad, parts):
        grads = jnp.split(grad, parts, axis=1)
        return [
            wide(lax.psum_scatter(g, ("dp", "seq"), scatter_dimension=0, tiled=True))
            for g in grads
        ]


def chain(state, through, reverse):
    count, mine = lax.axis_size("seq"), lax.axis_index("seq")
    entering = jnp.zeros_like(state)
    for hop in range(1, count):
        leaving = state if hop == 1 else state + through[..., None, None] * entering
        pair = (count - hop, count - 1 - hop) if reverse else (hop - 1, hop)
        entering = entering + wide(lax.ppermute(narrow(leaving), "seq", [pair]))
    return entering


def plain_body(
    inputs,
    lengths,
    first_gain,
    second_gain,
    query_weight,
    key_weight,
    value_weight,
    gate_weight,
    out_weight,
    up_weight,
    down_weight,
    out_cotangent,
):
    micro = inputs.shape[0]
    shard_len = inputs.shape[2]
    block_len = shard_len * lax.axis_size("tensor")
    block_start = lax.axis_index("seq") * block_len
    tensor_heads = query_weight.shape[1] // QK
    plan = Plain(tensor_heads)
    rows, heads = plan.rows, plan.heads
    head_index = (plan.first_head + jnp.arange(heads, dtype=jnp.int32)).astype(jnp.float32)
    log_gamma = jnp.log1p(-jnp.exp2(-5.0 - head_index))
    half_width = QK // 2
    gain_one = wide(first_gain)[:, None]
    gain_two = wide(second_gain)[:, None]
    row_lengths = plan.lengths(lengths)

    def scaled(weight, gain):
        return narrow(wide(weight) * gain)

    weight_qk = plan.gather_weight(
        scaled(query_weight, gain_one), scaled(key_weight, gain_one)
    )
    weight_v = plan.gather_weight(scaled(value_weight, gain_one))
    weight_g = plan.gather_weight(scaled(gate_weight, gain_one))
    weight_o = plan.gather_weight(out_weight)
    weight_d = plan.gather_weight(down_weight)
    weight_u = plan.gather_weight(scaled(up_weight, gain_two))
    width_q = weight_qk.shape[1] // 2

    def row_plan(lengths_row):
        documents, places = layout(lengths_row, block_start, block_len)
        previous, unused = layout(lengths_row, block_start - 1, 1)
        return (documents, places, previous[0])

    def forward(inputs_mb, lengths_mb, cotangent_mb):
        tokens = rows * block_len
        documents, places, previous = jax.vmap(row_plan)(lengths_mb)
        flat_places = places.reshape(-1)
        tables = [
            table.reshape(rows, block_len, 1, half_width)
            for sign in (1.0, -1.0)
            for table in rotation(flat_places, sign, QK)
        ]
        decay = jax.vmap(decay_parts, in_axes=(0, 0, None))(documents, previous, log_gamma)
        inner_decay, carried, leaving, through = decay
        carried_t = jnp.swapaxes(carried, 1, 2)[..., None]
        leaving_t = jnp.swapaxes(leaving, 1, 2)[..., None]
        residual = wide(inputs_mb)
        normed_first, inv_first = norm_rows(residual, EPSILON)
        hidden_first = plan.gather_tokens(narrow(normed_first))
        qk_pre = matmul(hidden_first, weight_qk)
        query_pre = qk_pre[:, :width_q].reshape(rows, block_len, heads, QK)
        key_pre = qk_pre[:, width_q:].reshape(rows, block_len, heads, QK)
        value_rows = narrow(matmul(hidden_first, weight_v)).reshape(rows, block_len, heads, HV)
        gate_pre = matmul(hidden_first, weight_g)
        queries = narrow(rotate(query_pre, tables[0], tables[1]))
        key_rows = narrow(rotate(key_pre, tables[2], tables[3]))
        score_matrix = einsum("rnhd,rmhd->rhnm", queries, key_rows)
        score_weights = narrow(score_matrix * inner_decay)
        intra_part = einsum("rhnm,rmhe->rnhe", score_weights, value_rows)
        decayed_keys = narrow(wide(key_rows) * leaving_t)
        block_state = einsum("rmhd,rmhe->rhde", decayed_keys, value_rows)
        state_in = narrow(chain(block_state, through, False))
        queries_carried = narrow(wide(queries) * carried_t)
        retained = intra_part + einsum("rnhd,rhde->rnhe", queries_carried, state_in)
        grouped, inv_group = norm_rows(retained, GROUP_EPSILON)
        grouped_flat = grouped.reshape(tokens, -1)
        mixed_rows = narrow(jax.nn.silu(gate_pre) * grouped_flat)
        middle = residual + plan.scatter_tokens(matmul_t(mixed_rows, weight_o))
        normed_second, inv_second = norm_rows(middle, EPSILON)
        hidden_second = plan.gather_tokens(narrow(normed_second))
        up_pre = matmul(hidden_second, weight_u)
        activated = narrow(gelu_exact(up_pre))
        outputs = narrow(middle + plan.scatter_tokens(matmul_t(activated, weight_d)))

        grad_rows = plan.gather_tokens(cotangent_mb)
        grad_act = matmul(grad_rows, weight_d)
        grad_up_pre = narrow(jax.vjp(gelu_exact, up_pre)[1](grad_act)[0])
        back_second = plan.scatter_tokens(matmul_t(grad_up_pre, weight_u))
        grad_middle = wide(cotangent_mb) + norm_back(back_second, normed_second, inv_second)
        grad_attn = plan.gather_tokens(narrow(grad_middle))
        grad_mixed = matmul(grad_attn, weight_o)
        grad_gate_pre = narrow(
            jax.vjp(jax.nn.silu, gate_pre)[1](grad_mixed * grouped_flat)[0]
        )
        grad_grouped = (grad_mixed * jax.nn.silu(gate_pre)).reshape(
            rows, block_len, heads, HV
        )
        grad_retained = narrow(norm_back(grad_grouped, grouped, inv_group))
        grad_scores = einsum("rnhe,rmhe->rhnm", grad_retained, value_rows)
        score_grads = narrow(grad_scores * inner_decay)
        direct = einsum("rnhd,rnhe->rhde", queries_carried, grad_retained)
        state_out = narrow(chain(direct, through, True))
        grad_queries = einsum("rhnm,rmhd->rnhd", score_grads, key_rows) + carried_t * einsum(
            "rnhe,rhde->rnhd", grad_retained, state_in
        )
        grad_keys = einsum("rhnm,rnhd->rmhd", score_grads, queries) + leaving_t * einsum(
            "rmhe,rhde->rmhd", value_rows, state_out
        )
        grad_values = einsum("rhnm,rnhe->rmhe", score_weights, grad_retained) + einsum(
            "rmhd,rhde->rmhe", decayed_keys, state_out
        )
        grad_query_pre = narrow(rotate_back(grad_queries, tables[0], tables[1]))
        grad_key_pre = narrow(rotate_back(grad_keys, tables[2], tables[3]))
        grad_qk_pre = jnp.concatenate(
            [grad_query_pre.reshape(tokens, -1), grad_key_pre.reshape(tokens, -1)], axis=1
        )
        grad_value_pre = narrow(grad_values).reshape(tokens, -1)
        first_part = matmul_t(grad_qk_pre, weight_qk) + matmul_t(grad_value_pre, weight_v)
        first_part = first_part + matmul_t(grad_gate_pre, weight_g)
        back_first = plan.scatter_tokens(first_part)
        grad_inputs = narrow(grad_middle + norm_back(back_first, normed_first, inv_first))
        pieces = (
            (hidden_first, grad_qk_pre),
            (hidden_first, grad_value_pre),
            (hidden_first, grad_gate_pre),
            (grad_attn, mixed_rows),
            (hidden_second, grad_up_pre),
            (grad_rows, activated),
        )
        return (outputs, grad_inputs, pieces)

    done = [
        forward(inputs[i, :, :, :].reshape(shard_len * inputs.shape[1], -1), row_lengths[i],
                out_cotangent[i].reshape(shard_len * inputs.shape[1], -1))
        for i in range(micro)
    ]

    def weight_grad(k):
        total = sum(tmatmul(*done[i][2][k]) for i in range(micro))
        return narrow(total)

    grad_down = plan.scatter_grad(weight_grad(5), 1)[0]
    grad_up = plan.scatter_grad(weight_grad(4), 1)[0]
    grad_out = plan.scatter_grad(weight_grad(3), 1)[0]
    grad_gate = plan.scatter_grad(weight_grad(2), 1)[0]
    grad_value = plan.scatter_grad(weight_grad(1), 1)[0]
    grad_query, grad_key = plan.scatter_grad(weight_grad(0), 2)

    def along(weight, grad):
        return jnp.sum(wide(weight) * grad, axis=1)

    gain_sums = lax.psum(
        (
            along(query_weight, grad_query)
            + along(key_weight, grad_key)
            + along(value_weight, grad_value)
            + along(gate_weight, grad_gate),
            along(up_weight, grad_up),
        ),
        "tensor",
    )
    shape = inputs.shape
    return (
        jnp.stack([d[0] for d in done]).reshape(shape),
        jnp.stack([d[1] for d in done]).reshape(shape),
        gain_sums[0],
        gain_sums[1],
        grad_query * gain_one,
        grad_key * gain_one,
        grad_value * gain_one,
        grad_gate * gain_one,
        grad_out,
        grad_up * gain_two,
        grad_down,
    )


def swap(values, axis, bit):
    return lax.ppermute(values, axis, [(i, i ^ bit) for i in range(lax.axis_size(axis))])


def in_order(mine, other, index, axis):
    return jnp.where(
        index == 0, jnp.stack([mine, other], axis), jnp.stack([other, mine], axis)
    )


LANES = 128


def group_of(place, upper):
    return lax.bitwise_xor(upper * 2, place)


def load_groups(ref, upper, groups):
    width = ref.shape[1] // groups
    parts = []
    for place in range(groups):
        at = pl.multiple_of(group_of(place, upper) * width, LANES)
        parts.append(ref[:, pl.ds(at, width)])
    return jnp.concatenate(parts, axis=1)


def store_groups(ref, values, upper, groups):
    width = ref.shape[1] // groups
    for place in range(groups):
        at = pl.multiple_of(group_of(place, upper) * width, LANES)
        ref[:, pl.ds(at, width)] = values[:, place * width : (place + 1) * width]


VMEM_BYTES = 48 << 20


def tied(values, *others):
    return lax.optimization_barrier((values,) + others)[0]


def join(*columns):
    rows, widths = sum(p.shape[0] for p in columns[0]), [c[0].shape[1] for c in columns]
    parts = [p for c in columns for p in c]
    count = max(1, 4 // len(parts))

    def kernel(*refs):
        ins, (out, held, arrived, left) = refs[: len(parts)], refs[len(parts) :]
        pieces, number, across = [], 0, 0
        for width, column in zip(widths, columns):
            at = 0
            for _ in column:
                ref = ins[number]
                number += 1
                size = ref.shape[0] // count
                for k in range(count):
                    i, place = len(pieces), (pl.ds(at, size), pl.ds(across, width))
                    pieces.append(
                        (
                            pltpu.make_async_copy(
                                ref.at[pl.ds(k * size, size)], held.at[place], arrived.at[i]
                            ),
                            pltpu.make_async_copy(held.at[place], out.at[place], left.at[i]),
                        )
                    )
                    at += size
            across += width
        for copy_in, copy_out in pieces:
            copy_in.start()
        for copy_in, copy_out in pieces:
            copy_in.wait()
            copy_out.start()
        for copy_in, copy_out in pieces:
            copy_out.wait()

    number = len(parts) * count
    shape, dtype = (rows, sum(widths)), parts[0].dtype
    return pl.pallas_call(
        kernel,
        out_shape=jax.ShapeDtypeStruct(shape, dtype),
        in_specs=[pl.BlockSpec(memory_space=pl.ANY)] * len(parts),
        out_specs=pl.BlockSpec(memory_space=pl.ANY),
        scratch_shapes=[
            pltpu.VMEM(shape, dtype),
            pltpu.SemaphoreType.DMA((number,)),
            pltpu.SemaphoreType.DMA((number,)),
        ],
        compiler_params=pltpu.CompilerParams(vmem_limit_bytes=VMEM_BYTES),
    )(*parts)


def call(kernel, grid, in_specs, out_specs, out_shape, scalars, *operands, aliases=()):
    return pl.pallas_call(
        kernel,
        out_shape=out_shape,
        grid_spec=pltpu.PrefetchScalarGridSpec(
            num_scalar_prefetch=len(scalars),
            grid=grid,
            in_specs=in_specs,
            out_specs=out_specs,
        ),
        compiler_params=pltpu.CompilerParams(
            dimension_semantics=("arbitrary",) * len(grid), vmem_limit_bytes=VMEM_BYTES
        ),
        input_output_aliases={len(scalars) + i: o for i, o in aliases},
    )(*scalars, *operands)


ROWS_STEP = 64


def row_call(kernel, upper, tokens, operands, out_types, first=(), into=None):
    features = operands[0].shape[1]
    starts = list(first) + [0] * (len(operands) - len(first))

    def spec(start):
        return pl.BlockSpec(
            (ROWS_STEP, features), lambda i, *_: (i + start // ROWS_STEP, 0)
        )

    ins = [spec(start) for start in starts]
    outs = [spec(0)] * len(out_types)
    shapes = [jax.ShapeDtypeStruct((tokens, features), t) for t in out_types]
    aliases = ()
    if into is not None:
        whole, at, rows = into
        outs = [spec(at)]
        shapes = [jax.ShapeDtypeStruct((rows, features), out_types[0])]
        if whole is not None:
            plain = kernel

            def kernel(*refs):
                plain(*refs[:-2], refs[-1])

            aliases = ((len(operands), 0),)
            operands = tuple(operands) + (whole,)
            ins.append(pl.BlockSpec(memory_space=pl.ANY))
    return call(
        kernel, (tokens // ROWS_STEP,), ins, outs, shapes, [upper], *operands, aliases=aliases
    )


def enter_tokens(upper, groups, tokens, start, inputs, cotangent):
    def kernel(up, x, c, normed, x_out, c_out):
        values = load_groups(x, up[0], groups)
        x_out[...] = values
        c_out[...] = load_groups(c, up[0], groups)
        normed[...] = narrow(norm_rows(wide(values), EPSILON)[0])

    return row_call(
        kernel, upper, tokens, (inputs, cotangent), (jnp.bfloat16,) * 3, (start, start)
    )


def total(parts):
    return sum(wide(p[...]) for p in parts)


def middle_tokens(upper, inputs, parts):
    def kernel(up, x, a, b, c, middle, normed):
        values = wide(x[...]) + total((a, b, c))
        middle[...] = values
        normed[...] = narrow(norm_rows(values, EPSILON)[0])

    return row_call(
        kernel, upper, inputs.shape[0], (inputs,) + parts, (jnp.float32, jnp.bfloat16)
    )


def output_tokens(upper, groups, middle, parts, into):
    def kernel(up, m, a, b, c, out):
        store_groups(out, narrow(m[...] + total((a, b, c))), up[0], groups)

    return row_call(
        kernel, upper, middle.shape[0], (middle,) + parts, (jnp.bfloat16,), into=into
    )[0]


def back_middle(upper, middle, cotangent, parts):
    def kernel(up, m, g, a, b, c, grad, grad_narrow):
        normed, inv = norm_rows(m[...], EPSILON)
        values = wide(g[...]) + norm_back(total((a, b, c)), normed, inv)
        grad[...] = values
        grad_narrow[...] = narrow(values)

    return row_call(
        kernel,
        upper,
        middle.shape[0],
        (middle, cotangent) + parts,
        (jnp.float32, jnp.bfloat16),
    )


def back_inputs(upper, groups, inputs, grad_middle, parts, into):
    def kernel(up, x, g, a, b, c, out):
        normed, inv = norm_rows(wide(x[...]), EPSILON)
        values = g[...] + norm_back(total((a, b, c)), normed, inv)
        store_groups(out, narrow(values), up[0], groups)

    return row_call(
        kernel,
        upper,
        inputs.shape[0],
        (inputs, grad_middle) + parts,
        (jnp.bfloat16,),
        into=into,
    )[0]


def dot(left, right, left_dim, right_dim):
    return lax.dot_general(
        left, right, (((left_dim,), (right_dim,)), ((), ())), preferred_element_type=jnp.float32
    )


class Retention:
    def __init__(self, plan, log_gamma, core, documents, previous, tables):
        rows, length = documents.shape
        self.rows, self.heads, self.length = rows, plan.heads, length
        self.q_wide, self.v_wide = plan.heads * QK, plan.heads * HV
        last = documents[:, -1]
        self.scalars = [
            jnp.concatenate([core[None], previous, last]).astype(jnp.int32),
            log_gamma,
        ]
        self.documents = [documents[:, :, None], documents[:, None, :]]
        self.tables = tables

    def token_spec(self, width):
        return pl.BlockSpec(
            (2, None, self.length // 2, width), lambda r, *_: (0, r, 0, 0)
        )

    def head_spec(self, *shape):
        return pl.BlockSpec(
            (None, self.heads) + shape, lambda r, *_: (r, 0) + (0,) * len(shape)
        )

    def row_spec(self, *shape):
        return pl.BlockSpec((None,) + shape, lambda r, *_: (r,) + (0,) * len(shape))

    def token_type(self, width, dtype=jnp.bfloat16):
        return jax.ShapeDtypeStruct((2, self.rows, self.length // 2, width), dtype)

    def head_type(self, *shape, dtype=jnp.bfloat16):
        return jax.ShapeDtypeStruct((self.rows, self.heads) + shape, dtype)

    def tokens(self, values):
        return values.reshape(2, self.rows, self.length // 2, -1)

    def document_specs(self):
        return [self.row_spec(self.length, 1), self.row_spec(1, self.length)]

    def table_specs(self):
        return [self.row_spec(self.length, QK // 2)] * 2

    def run(self, kernel, in_specs, out, operands):
        return call(
            kernel,
            (self.rows,),
            in_specs,
            [spec for spec, shape in out],
            [shape for spec, shape in out],
            self.scalars,
            *operands,
        )

    def load(self, ref, core, at, width):
        return jnp.concatenate(
            [ref[core, :, at : at + width], ref[1 - core, :, at : at + width]], axis=0
        )

    def store(self, ref, core, at, values):
        half, width = self.length // 2, values.shape[1]
        ref[core, :, at : at + width] = values[:half]
        ref[1 - core, :, at : at + width] = values[half:]

    def carried(self, numbers, log_gamma, docs, row, head):
        steps = wide(lax.broadcasted_iota(jnp.int32, (self.length, 1), 0))
        kept = jnp.exp((steps + 1.0) * log_gamma[head])
        return jnp.where(docs[...] == numbers[1 + row], kept, 0.0)

    def leaving(self, numbers, log_gamma, docs, row, head):
        steps = wide(lax.broadcasted_iota(jnp.int32, (self.length, 1), 0))
        kept = jnp.exp((self.length - 1.0 - steps) * log_gamma[head])
        return jnp.where(docs[...] == numbers[1 + self.rows + row], kept, 0.0)

    def inner(self, log_gamma, docs, docs_t, head):
        shape = (self.length, self.length)
        distance = wide(
            lax.broadcasted_iota(jnp.int32, shape, 0) - lax.broadcasted_iota(jnp.int32, shape, 1)
        )
        kept = jnp.exp(jnp.maximum(distance, 0.0) * log_gamma[head])
        return jnp.where((docs[...] == docs_t[...]) & (distance >= 0.0), kept, 0.0)

    def retained(self, numbers, log_gamma, docs, docs_t, row, head, query, key, value, state):
        inner = self.inner(log_gamma, docs, docs_t, head)
        weights = narrow(dot(query, key, 1, 1) * inner)
        carried = self.carried(numbers, log_gamma, docs, row, head)
        values = dot(weights, value, 1, 0) + carried * dot(query, state, 1, 0)
        grouped, inv = norm_rows(values, GROUP_EPSILON)
        return inner, weights, carried, grouped, inv

    def keys(self, kv_pre):
        def kernel(numbers, log_gamma, kv, docs, docs_t, cos, sin, keys, values, state):
            row, core = pl.program_id(0), numbers[0]
            for head in range(self.heads):
                key = self.load(kv, core, head * QK, QK)
                key = narrow(rotate(key, cos[...], sin[...]))
                value = narrow(self.load(kv, core, self.q_wide + head * HV, HV))
                leaving = self.leaving(numbers, log_gamma, docs, row, head)
                keys[head] = key
                values[head] = value
                state[head] = narrow(dot(narrow(wide(key) * leaving), value, 0, 0))

        n = self.length
        return self.run(
            kernel,
            [self.token_spec(self.q_wide + self.v_wide)] + self.document_specs() + self.table_specs(),
            [
                (self.head_spec(n, QK), self.head_type(n, QK)),
                (self.head_spec(n, HV), self.head_type(n, HV)),
                (self.head_spec(QK, HV), self.head_type(QK, HV)),
            ],
            [self.tokens(kv_pre)] + self.documents + self.tables[2:],
        )

    def mix(self, qg_pre, keys, values, state_in):
        def kernel(
            numbers, log_gamma, qg, key_ref, value_ref, state_ref, docs, docs_t, cos, sin,
            queries, mixed,
        ):
            row, core = pl.program_id(0), numbers[0]
            for head in range(self.heads):
                query = self.load(qg, core, head * QK, QK)
                query = narrow(rotate(query, cos[...], sin[...]))
                queries[head] = query
                grouped = self.retained(
                    numbers, log_gamma, docs, docs_t, row, head,
                    query, key_ref[head], value_ref[head], state_ref[head],
                )[3]
                gate = self.load(qg, core, self.q_wide + head * HV, HV)
                out = narrow(gate * jax.nn.sigmoid(gate) * grouped)
                self.store(mixed, core, head * HV, out)

        n = self.length
        queries, mixed = self.run(
            kernel,
            [
                self.token_spec(self.q_wide + self.v_wide),
                self.head_spec(n, QK),
                self.head_spec(n, HV),
                self.head_spec(QK, HV),
            ]
            + self.document_specs()
            + self.table_specs(),
            [
                (self.head_spec(n, QK), self.head_type(n, QK)),
                (self.token_spec(self.v_wide), self.token_type(self.v_wide)),
            ],
            [self.tokens(qg_pre), keys, values, state_in] + self.documents + self.tables[:2],
        )
        return queries, mixed.reshape(-1, self.v_wide)

    def back(self, qg_pre, grad_mixed, queries, keys, values, state_in):
        def kernel(
            numbers, log_gamma, qg, grad_ref, query_ref, key_ref, value_ref, state_ref,
            docs, docs_t, cos, sin, grad_qg, direct, grad_keys, grad_values,
        ):
            row, core = pl.program_id(0), numbers[0]
            for head in range(self.heads):
                query, key, value = query_ref[head], key_ref[head], value_ref[head]
                state = state_ref[head]
                inner, weights, carried, grouped, inv = self.retained(
                    numbers, log_gamma, docs, docs_t, row, head, query, key, value, state
                )
                gate = self.load(qg, core, self.q_wide + head * HV, HV)
                grad = self.load(grad_ref, core, head * HV, HV)
                sigmoid = jax.nn.sigmoid(gate)
                grad_gate = grad * grouped * (sigmoid * (1.0 + gate * (1.0 - sigmoid)))
                self.store(grad_qg, core, self.q_wide + head * HV, narrow(grad_gate))
                grad_retained = narrow(norm_back(grad * (gate * sigmoid), grouped, inv))
                score_grads = narrow(dot(grad_retained, value, 1, 1) * inner)
                direct[head] = narrow(
                    dot(narrow(wide(query) * carried), grad_retained, 0, 0)
                )
                grad_query = dot(score_grads, key, 1, 0) + carried * dot(
                    grad_retained, state, 1, 1
                )
                grad_query = rotate_back(grad_query, cos[...], sin[...])
                self.store(grad_qg, core, head * QK, narrow(grad_query))
                grad_keys[head] = dot(score_grads, query, 0, 0)
                grad_values[head] = dot(weights, grad_retained, 0, 0)

        n = self.length
        wide_all = self.q_wide + self.v_wide
        return self.run(
            kernel,
            [
                self.token_spec(wide_all),
                self.token_spec(self.v_wide),
                self.head_spec(n, QK),
                self.head_spec(n, QK),
                self.head_spec(n, HV),
                self.head_spec(QK, HV),
            ]
            + self.document_specs()
            + self.table_specs(),
            [
                (self.token_spec(wide_all), self.token_type(wide_all)),
                (self.head_spec(QK, HV), self.head_type(QK, HV)),
                (self.head_spec(n, QK), self.head_type(n, QK, dtype=jnp.float32)),
                (self.head_spec(n, HV), self.head_type(n, HV, dtype=jnp.float32)),
            ],
            [self.tokens(qg_pre), self.tokens(grad_mixed), queries, keys, values, state_in]
            + self.documents
            + self.tables[:2],
        )

    def back_keys(self, keys, values, state_out, grad_keys, grad_values):
        def kernel(
            numbers, log_gamma, key_ref, value_ref, state_ref, key_part, value_part,
            docs, docs_t, cos, sin, grad_kv,
        ):
            row, core = pl.program_id(0), numbers[0]
            for head in range(self.heads):
                leaving = self.leaving(numbers, log_gamma, docs, row, head)
                state = state_ref[head]
                grad_key = key_part[head] + leaving * dot(value_ref[head], state, 1, 1)
                grad_key = rotate_back(grad_key, cos[...], sin[...])
                self.store(grad_kv, core, head * QK, narrow(grad_key))
                grad_value = value_part[head] + leaving * dot(key_ref[head], state, 1, 0)
                self.store(grad_kv, core, self.q_wide + head * HV, narrow(grad_value))

        n = self.length
        wide_all = self.q_wide + self.v_wide
        return self.run(
            kernel,
            [
                self.head_spec(n, QK),
                self.head_spec(n, HV),
                self.head_spec(QK, HV),
                self.head_spec(n, QK),
                self.head_spec(n, HV),
            ]
            + self.document_specs()
            + self.table_specs(),
            [(self.token_spec(wide_all), self.token_type(wide_all))],
            [keys, values, state_out, grad_keys, grad_values] + self.documents + self.tables[2:],
        )[0].reshape(-1, wide_all)


class Paired:
    def __init__(self, tensor_heads):
        self.rows = 2
        self.heads = tensor_heads // 2
        self.block = lax.axis_index("seq").astype(jnp.int32)
        self.side = self.block % 2
        self.upper = self.block // 2
        self.core = lax.axis_index("tensor")
        self.groups = lax.axis_size("dp") * lax.axis_size("seq")
        self.first_head = self.core * tensor_heads + self.side * self.heads

    def gather_tokens(self, values, *before):
        return self.gather_from(values, tied(swap(values, "seq", 1), *before))

    def gather_from(self, values, across):
        own = (values, swap(values, "tensor", 1))
        return join((own[0], across, own[1], swap(across, "tensor", 1)))

    def scatter_tokens(self, product):
        away = swap(product(1), "tensor", 1)
        here = product(0)
        half = here.shape[0] // 2
        across = narrow(wide(here[half:]) + wide(away[half:]))
        return (here[:half], away[:half], swap(across, "seq", 1)), here, across

    def halves(self, shard, which):
        width = shard.shape[1] // 2
        return lax.dynamic_slice_in_dim(shard, which * width, width, 1)

    def swap_weight(self, shards, *before):
        here = jnp.concatenate([self.halves(w, self.side) for w in shards], axis=1)
        away = jnp.concatenate([self.halves(w, 1 - self.side) for w in shards], axis=1)
        return here, swap(tied(away, *before), "seq", 1)

    def pair_weight(self, here, across):
        return in_order(here, across, self.side, 0).reshape(-1, here.shape[1])

    def spread_weight(self, two, far):
        return lax.all_gather(jnp.concatenate([two, far]), "dp", axis=0, tiled=True)

    def collect_grad(self, product, *before):
        return lax.psum_scatter(tied(product, *before), "dp", scatter_dimension=0, tiled=True)

    def scatter_grad(self, fours, widths):
        mine, other = [], []
        for four in fours:
            half = four.shape[0] // 2
            two = wide(four[:half]) + wide(swap(four[half:], "seq", 2))
            two = two.reshape(2, -1, four.shape[1])
            away = narrow(lax.dynamic_index_in_dim(two, 1 - self.side, 0, False))
            mine.append(lax.dynamic_index_in_dim(two, self.side, 0, False))
            other.append(wide(swap(away, "seq", 1)))
        mine, other = jnp.concatenate(mine, axis=1), jnp.concatenate(other, axis=1)
        out, at = [], 0
        for width in widths:
            part = in_order(mine[:, at : at + width], other[:, at : at + width], self.side, 1)
            out.append(part.reshape(mine.shape[0], -1))
            at += width
        return out

    def in_blocks(self, values):
        first = jnp.where(self.side == 0, values[0], values[1])
        return first, jnp.where(self.side == 0, values[1], values[0])

    def own_first(self, earlier, later):
        return in_order(earlier, later, self.side, 0)

    def states(self, own, through, reverse):
        early, late = self.in_blocks(own)
        kept_early, kept_late = self.in_blocks(through[..., None, None])
        if reverse:
            early, late, kept_early, kept_late = late, early, kept_late, kept_early
        leaving = narrow(wide(late) + kept_late * wide(early))
        hops = [(2, 0), (3, 1)] if reverse else [(0, 2), (1, 3)]
        return (early, kept_early), leaving, lax.ppermute(leaving, "seq", hops)

    def arrive(self, early, entering, reverse, *before):
        state, kept = early
        entering = tied(entering, *before)
        inner = narrow(wide(state) + kept * wide(entering))
        pair = (inner, entering) if reverse else (entering, inner)
        return self.own_first(*pair)


def paired_body(
    inputs,
    lengths,
    first_gain,
    second_gain,
    query_weight,
    key_weight,
    value_weight,
    gate_weight,
    out_weight,
    up_weight,
    down_weight,
    out_cotangent,
):
    micro = inputs.shape[0]
    shard_len, features = inputs.shape[2:]
    block_len = shard_len * 2
    plan = Paired(query_weight.shape[1] // QK)
    rows, heads, groups = plan.rows, plan.heads, plan.groups
    starts = jnp.stack([plan.block, lax.bitwise_xor(plan.block, 1)]) * block_len
    upper = plan.upper[None]
    head_index = (plan.first_head + jnp.arange(heads, dtype=jnp.int32)).astype(jnp.float32)
    log_gamma = jnp.log1p(-jnp.exp2(-5.0 - head_index))
    gain_one = wide(first_gain)[:, None]
    gain_two = wide(second_gain)[:, None]

    def scaled(weight, gain):
        return narrow(wide(weight) * gain)

    flat = (micro * shard_len, features)
    units = [
        (scaled(key_weight, gain_one), scaled(value_weight, gain_one)),
        (scaled(query_weight, gain_one), scaled(gate_weight, gain_one)),
        (out_weight,),
        (down_weight,),
        (scaled(up_weight, gain_two),),
    ]
    here, across = plan.swap_weight(units[0])
    entered = [
        enter_tokens(
            upper,
            groups,
            shard_len,
            i * shard_len,
            inputs.reshape(flat),
            out_cotangent.reshape(flat),
        )
        for i in range(micro)
    ]
    across = tied(across, *[e[0] for e in entered])

    def far(two, *before):
        return swap(tied(two, *before), "seq", 2)

    first_across = [swap(e[0], "seq", 1) for e in entered]
    cot_across = [swap(e[2], "seq", 1) for e in entered]
    two_kv = plan.pair_weight(here, across)
    weight_kv = plan.spread_weight(two_kv, tied(far(two_kv), first_across[0]))
    two_qg = plan.pair_weight(*plan.swap_weight(units[1], two_kv))
    far_qg = tied(far(two_qg), first_across[1])
    weight_qg = plan.spread_weight(two_qg, far_qg)
    hidden_first = [plan.gather_from(e[0], a) for e, a in zip(entered, first_across)]
    two_o = plan.pair_weight(*plan.swap_weight(units[2], far_qg))

    def row_plan(start, lengths_row):
        documents, places = layout(lengths_row, start, block_len)
        previous, unused = layout(lengths_row, start - 1, 1)
        return (documents, places, previous[0])

    kernels, throughs = [], []
    for i in range(micro):
        documents, places, previous = jax.vmap(row_plan, in_axes=(0, None))(
            starts, lengths[i, 0]
        )
        tables = [
            table.reshape(rows, block_len, QK // 2)
            for sign in (1.0, -1.0)
            for table in rotation(places.reshape(-1), sign, QK)
        ]
        kernels.append(Retention(plan, log_gamma, plan.core, documents, previous, tables))
        throughs.append(
            jnp.where(
                (previous == documents[:, -1])[:, None], jnp.exp(block_len * log_gamma)[None], 0.0
            )
        )

    each = range(micro)
    half = rows * shard_len

    def rows_of(values, away):
        return values[half:] if away else values[:half]

    def product_t(values, weight):
        return lambda away: narrow(matmul_t(rows_of(values, away), weight))

    def product(left, right, columns=slice(None)):
        return narrow(sum(tmatmul(left[i], right[i][:, columns]) for i in each))

    kv_pre = [matmul(hidden_first[i], weight_kv) for i in each]
    kvs = [kernels[0].keys(kv_pre[0])]
    kv_pre[1] = tied(kv_pre[1], kvs[0][2])
    kvs.append(kernels[1].keys(kv_pre[1]))
    passing = [plan.states(kvs[i][2], throughs[i], False) for i in each]
    far_o = tied(far(two_o), kvs[1][2], cot_across[0])
    weight_o = plan.spread_weight(two_o, far_o)
    two_d = plan.pair_weight(*plan.swap_weight(units[3], far_o))
    qg_pre = [matmul(tied(hidden_first[i], two_d), weight_qg) for i in each]
    far_d = tied(far(two_d), qg_pre[1], cot_across[1])
    weight_d = plan.spread_weight(two_d, far_d)
    two_u = plan.pair_weight(*plan.swap_weight(units[4], far_d))
    grad_rows = [plan.gather_from(e[2], a) for e, a in zip(entered, cot_across)]

    def held(parts, *before):
        return (parts[0], parts[1], tied(parts[2], *before))

    mixes, attn, state_in = [], [], []
    for i in each:
        early, leaving, entering = passing[i]
        state_in.append(plan.arrive(early, entering, False, two_u))
        mixes.append(kernels[i].mix(qg_pre[i], kvs[i][0], kvs[i][1], state_in[i]))
    far_u = tied(far(two_u), mixes[1][1])
    weight_u = plan.spread_weight(two_u, far_u)
    before = (far_u,)
    for i in each:
        source = tied(mixes[i][1], *before)
        parts, here, across = plan.scatter_tokens(product_t(source, weight_o))
        attn.append(parts)
        before = (across,)
    middles = [middle_tokens(upper, entered[0][1], attn[0])]
    grad_act = [matmul(grad_rows[i], weight_d) for i in each]
    hidden_second, activated, grad_up_pre, second = [], [], [], []
    before = ()
    for i in each:
        if i:
            attn[1] = held(attn[1], *before)
            middles.append(middle_tokens(upper, entered[1][1], attn[1]))
        hidden_second.append(plan.gather_tokens(middles[i][1]))
        source = tied(hidden_second[i], *((across,) if i else grad_act))
        up_pre = matmul(source, weight_u)
        activated.append(narrow(gelu_exact(up_pre)))
        grad_up_pre.append(narrow(jax.vjp(gelu_exact, up_pre)[1](grad_act[i])[0]))
        if i:
            second[0] = held(second[0], activated[1])
            grad_middle = [back_middle(upper, middles[0][0], entered[0][2], second[0])]
            towards = product_t(tied(grad_up_pre[1], grad_middle[0][1]), weight_u)
        else:
            towards = product_t(grad_up_pre[0], weight_u)
        parts, here, across = plan.scatter_tokens(towards)
        second.append(parts)
        before = (here,)
    down_product = product(grad_rows, [tied(a, here) for a in activated])
    down_four = plan.collect_grad(down_product)
    grad_attn = [plan.gather_tokens(grad_middle[0][1], down_product)]
    grad_mixed = matmul(grad_attn[0], weight_o)
    second[1] = held(second[1], grad_mixed)
    grad_middle.append(back_middle(upper, middles[1][0], entered[1][2], second[1]))
    backs = []
    for i in each:
        kv = kvs[i]
        source = tied(grad_mixed, down_four if i else grad_middle[1][1])
        backs.append(
            kernels[i].back(qg_pre[i], source, mixes[i][0], kv[0], kv[1], state_in[i])
        )
        if not i:
            up_product = product(
                hidden_second, [tied(g, backs[0][1]) for g in grad_up_pre]
            )
            grad_attn.append(plan.gather_tokens(grad_middle[1][1], up_product))
            grad_mixed = matmul(grad_attn[1], weight_o)
    after_back = backs[-1][1]
    up_four = plan.collect_grad(up_product)
    grad_qg_pre = [b[0].reshape(-1, b[0].shape[-1]) for b in backs]
    passing = [plan.states(backs[i][1], throughs[i], True) for i in each]
    out_product = product(grad_attn, [tied(m[1], after_back) for m in mixes])
    out_four = plan.collect_grad(out_product)
    qg_product = product(hidden_first, [tied(g, out_product) for g in grad_qg_pre])
    qg_four = plan.collect_grad(qg_product)
    state_out = []
    before = (qg_product, up_four)
    for i in each:
        early, leaving, entering = passing[i]
        state_out.append(plan.arrive(early, entering, True, *before))
    late = [tied(a, qg_product) for a in activated]
    ffn = [plan.scatter_tokens(product_t(late[i], weight_d)) for i in each]
    outputs = grad_inputs = None
    for i in each:
        into = (outputs, i * shard_len, flat[0])
        outputs = output_tokens(upper, groups, middles[i][0], ffn[i][0], into)
    grad_kv_pre = [
        kernels[i].back_keys(kvs[i][0], kvs[i][1], state_out[i], backs[i][2], backs[i][3])
        for i in each
    ]
    cut = grad_kv_pre[0].shape[1] // 2
    kv_products = [
        product(hidden_first, grad_kv_pre, columns)
        for columns in (slice(None, cut), slice(cut, None))
    ]
    kv_fours = [
        plan.collect_grad(kv_products[0], out_four),
        plan.collect_grad(kv_products[1], qg_four),
    ]
    first = []
    for i in each:
        first_kv = tied(grad_kv_pre[i], *kv_products)

        def first_product(away):
            part = matmul_t(rows_of(grad_qg_pre[i], away), weight_qg)
            return narrow(part + matmul_t(rows_of(first_kv, away), weight_kv))

        first.append(plan.scatter_tokens(first_product)[0])
    for i in each:
        into = (grad_inputs, i * shard_len, flat[0])
        grad_inputs = back_inputs(
            upper, groups, entered[i][1], grad_middle[i][0], first[i], into
        )

    width_q, width_v = heads * QK, heads * HV
    width_f = up_weight.shape[1] // 2

    wide_four = jnp.concatenate([down_four, up_four, out_four], axis=1)
    grad_down, grad_up, grad_out = plan.scatter_grad([wide_four], [width_f, width_f, width_v])
    grad_query, grad_gate = plan.scatter_grad([qg_four], [width_q, width_v])
    grad_key, grad_value = plan.scatter_grad(
        [jnp.concatenate(kv_fours, axis=1)], [width_q, width_v]
    )

    def along(weight, grad):
        return jnp.sum(wide(weight) * grad, axis=1)

    gain_sums = lax.psum(
        (
            along(query_weight, grad_query)
            + along(key_weight, grad_key)
            + along(value_weight, grad_value)
            + along(gate_weight, grad_gate),
            along(up_weight, grad_up),
        ),
        "tensor",
    )
    return (
        outputs.reshape(inputs.shape),
        grad_inputs.reshape(inputs.shape),
        gain_sums[0],
        gain_sums[1],
        grad_query * gain_one,
        grad_key * gain_one,
        grad_value * gain_one,
        grad_gate * gain_one,
        grad_out,
        grad_up * gain_two,
        grad_down,
    )


def body(inputs, lengths, first_gain, second_gain, query_weight, *rest):
    paired = (
        lax.axis_size("seq") == 4
        and lax.axis_size("tensor") == 2
        and inputs.shape[1] == 1
        and query_weight.shape[1] % (2 * QK) == 0
        and query_weight.shape[0] % LANES == 0
        and inputs.shape[2] % ROWS_STEP == 0
    )
    run = paired_body if paired else plain_body
    return run(inputs, lengths, first_gain, second_gain, query_weight, *rest)


def solution(mesh):
    tokens = P(None, "dp", ("seq", "tensor"), None)
    vector = P(("dp", "seq"))
    matrix = P(("dp", "seq"), "tensor")
    return jax.shard_map(
        body,
        mesh=mesh,
        in_specs=(tokens, P(None, "dp", None), vector, vector) + (matrix,) * 7 + (tokens,),
        out_specs=(tokens, tokens, vector, vector) + (matrix,) * 7,
        check_vma=False,
    )
```
